32 devices in a mesh: gx: 4 (over x, core), gy: 8 (over z, y).
Axes of the slice: x: 2, y: 2, z: 4, core: 2. Of those that a mesh axis runs over, the one named last changes fastest.
Arguments:
- field: float32 [12, 64, 64, 128], P(None, 'gx', 'gy'), may hold values from -16 to 16
- diffusion: float32 [12], replicated, may hold values from 0.02 to 0.15
- prefactor: float32 [12], replicated, may hold values from 0.05 to 0.3
- activation: float32 [12], replicated, may hold values from 0.5 to 2
- mixing: float32 [12, 12], replicated, may hold values from -1.75 to 1.75
- basis_x: float32 [64, 64], P('gx'), may hold values from -1 to 1, as said below
- basis_y: float32 [64, 64], P('gy'), may hold values from -1 to 1, as said below
- basis_z: float32 [128, 32], replicated, may hold values from -1 to 1, as said below
- basis_v: float32 [12, 6], replicated, may hold values from -1 to 1, as said below
Outputs:
- state: float32 [12, 64, 64, 128], P(None, 'gx', 'gy')
- recon: float32 [12, 64, 64, 128], P(None, 'gx', 'gy')
- residual: float32 [12], replicated
The draws below stay inside these ranges and needn't reach their ends.
Inputs may be any that keep to these rules, and one draw needn't show every extreme that they name: `basis_x`: its 64 columns are mutually orthogonal, each of norm between 0.5 and 1. `basis_y`: its 64 columns are orthonormal. `basis_z`: its 32 columns are orthonormal. `basis_v`: its 6 columns are orthonormal.
All inputs are finite; a program needn't handle non-finite values.
Results may differ from the reference program's by a relative error of at most 0.00013.
Values sent between devices are 32-bit elements; how exact they have to be, the bound alone decides.
No kernel may reach another device: no remote copies, remote signals or barrier semaphores. Data moves between devices by JAX's collectives and lax.ppermute only.
A program may use at most 64 MiB of HBM per device.

```python
import math
import jax
import jax.numpy as jnp
from jax import lax

NZ = 128
VARS = 12
RX = 64
RY = 64
RZ = 32
RV = 6
STEPS = 1
NX = 64
NY = 64


HIGH = lax.Precision.HIGHEST


def orthonormal(key, count_rows, count_cols, row_scale):
    sample_matrix = jax.random.normal(key, (count_rows, count_cols), jnp.float32) * row_scale[:, None]
    factor, unused = jnp.linalg.qr(sample_matrix)
    return factor.astype(jnp.float32)


def grid_positions():
    x_pos = jnp.arange(NX, dtype=jnp.float32) / max(NX - 1, 1)
    y_pos = jnp.arange(NY, dtype=jnp.float32) / max(NY - 1, 1)
    return (x_pos, y_pos)


def tucker_factors(key):
    streams = jax.random.split(jax.random.fold_in(key, 101), 5)
    x_pos, y_pos = grid_positions()
    grow_x = jnp.exp(0.5 * math.log(3.0) * x_pos)
    grow_y = jnp.exp(0.5 * math.log(3.0) * y_pos)
    column_norms = jnp.exp(jax.random.uniform(streams[4], (RX,), jnp.float32, math.log(0.5), 0.0))
    factor_x = orthonormal(streams[0], NX, RX, grow_x) * column_norms[None, :]
    factor_y = orthonormal(streams[1], NY, RY, grow_y)
    factor_z = orthonormal(streams[2], NZ, RZ, jnp.ones((NZ,), jnp.float32))
    factor_v = orthonormal(streams[3], VARS, RV, jnp.ones((VARS,), jnp.float32))
    return (factor_x, factor_y, factor_z, factor_v)


def draw_basis_x(key, part):
    return tucker_factors(key)[0]


def draw_basis_y(key, part):
    return tucker_factors(key)[1]


def draw_basis_z(key, part):
    return tucker_factors(key)[2]


def draw_basis_v(key, part):
    return tucker_factors(key)[3]


def draw_field(key, part):
    factor_x, factor_y, factor_z, factor_v = tucker_factors(key)
    streams = jax.random.split(jax.random.fold_in(key, 11), 4)
    x_pos, y_pos = grid_positions()
    amplitude = 0.4 * math.sqrt(NX * NY * NZ * VARS / (RX * RY * RZ * RV))
    core = jax.random.normal(streams[0], (RX, RY, RZ, RV), jnp.float32)
    noise = jax.random.normal(streams[1], (VARS, NX, NY, NZ), jnp.float32)
    levels = jnp.exp(jax.random.uniform(streams[2], (VARS,), jnp.float32, math.log(0.03), math.log(1.0)))
    smooth = jnp.zeros((NX, NY), jnp.float32)
    rough = jax.random.uniform(streams[3], (VARS, NX, NY, NZ), jnp.float32, 0.5, 1.5)
    core = core * amplitude
    mixed_v = jnp.einsum('abrs,vs->abrv', core, factor_v, precision=HIGH)
    mixed_z = jnp.einsum('abrv,zr->abzv', mixed_v, factor_z, precision=HIGH)
    mixed_y = jnp.einsum('abzv,yb->ayzv', mixed_z, factor_y, precision=HIGH)
    tucker = jnp.einsum('ayzv,xa->vxyz', mixed_y, factor_x, precision=HIGH)
    fade = jnp.exp(-0.5 * math.log(3.0) * (x_pos[:, None] + y_pos[None, :]))
    noise_part = 0.4 * levels[:, None, None, None] * fade[None, :, :, None] * rough * noise
    values = tucker + noise_part + smooth[None, :, :, None]
    return jnp.clip(values, -16.0, 16.0).astype(jnp.float32)


def centred(rng, shape, spread, limit, kind=jnp.bfloat16):
    entries = spread * jax.random.normal(rng, shape, jnp.float32)
    return jnp.clip(entries, min=-limit, max=limit).astype(kind)


def setup_inputs(seed: int = 0) -> dict:
    key_list = jax.random.split(jax.random.key(seed), 10)
    return {
        "field": draw_field(jax.random.fold_in(key_list[9], 71), 0),
        "diffusion": jnp.clip(jnp.exp(jax.random.uniform(key_list[1], (VARS,), jnp.float32, math.log(0.02), math.log(0.15))), 0.02, 0.15),
        "prefactor": jnp.clip(jnp.exp(jax.random.uniform(key_list[2], (VARS,), jnp.float32, math.log(0.05), math.log(0.3))), 0.05, 0.3),
        "activation": jnp.clip(jax.random.uniform(key_list[3], (VARS,), jnp.float32, 0.5, 2.0), 0.5, 2.0),
        "mixing": centred(key_list[4], (VARS, VARS), VARS ** -0.5, 1.75, jnp.float32),
        "basis_x": draw_basis_x(jax.random.fold_in(key_list[9], 71), 0),
        "basis_y": draw_basis_y(jax.random.fold_in(key_list[9], 71), 0),
        "basis_z": draw_basis_z(jax.random.fold_in(key_list[9], 71), 0),
        "basis_v": draw_basis_v(jax.random.fold_in(key_list[9], 71), 0),
    }


HIGH = lax.Precision.HIGHEST

def lap_core(padded):
    centre = padded[:, 1:-1, 1:-1, 1:-1]
    summed = padded[:, 2:, 1:-1, 1:-1] + padded[:, :-2, 1:-1, 1:-1]
    summed = summed + padded[:, 1:-1, 2:, 1:-1] + padded[:, 1:-1, :-2, 1:-1]
    summed = summed + padded[:, 1:-1, 1:-1, 2:] + padded[:, 1:-1, 1:-1, :-2]
    return summed - 6.0 * centre

def reaction(centre, prefactor, activation, mixing):
    temper = 1.5 + jnp.tanh(centre[0])
    rate_terms = prefactor[:, None, None, None] * jnp.exp(-activation[:, None, None, None] / temper[None]) * centre
    return jnp.einsum('vw,wxyz->vxyz', mixing, rate_terms, precision=HIGH)

def tendency(centre, diffusion, prefactor, activation, mixing):
    padded = jnp.pad(centre, ((0, 0), (1, 1), (1, 1), (1, 1)))
    return diffusion[:, None, None, None] * lap_core(padded) + reaction(centre, prefactor, activation, mixing)

def reference(field, diffusion, prefactor, activation, mixing, basis_x, basis_y, basis_z, basis_v):
    state = field
    for step_index in range(STEPS):
        section = state + tendency(state, diffusion, prefactor, activation, mixing)
        state = 0.5 * (state + section + tendency(section, diffusion, prefactor, activation, mixing))
    proj_z = jnp.einsum('vxyz,zr->vxyr', state, basis_z, precision=HIGH)
    packed = jnp.einsum('vxyr,vs->xyrs', proj_z, basis_v, precision=HIGH)
    packed = packed.reshape(NX, NY, RZ * RV)
    part_x = jnp.einsum('xa,xyk->ayk', basis_x, packed, precision=HIGH)
    core = jnp.einsum('ayk,yb->abk', part_x, basis_y, precision=HIGH)
    mixed_y = jnp.einsum('abk,yb->ayk', core, basis_y, precision=HIGH)
    decoded = jnp.einsum('xa,ayk->xyk', basis_x, mixed_y, precision=HIGH)
    decoded = decoded.reshape(NX, NY, RZ, RV)
    back_v = jnp.einsum('xyrs,vs->vxyr', decoded, basis_v, precision=HIGH)
    recon = jnp.einsum('vxyr,zr->vxyz', back_v, basis_z, precision=HIGH)
    error = state - recon
    miss = lax.optimization_barrier(jnp.sum(error * error, axis=(1, 2, 3)))
    mass = lax.optimization_barrier(jnp.sum(state * state, axis=(1, 2, 3)))
    residual = jnp.sqrt(miss / (mass + 1e-06))
    return (state, recon, residual)
```

```python
import jax
import jax.numpy as jnp
from jax import lax
from jax.sharding import PartitionSpec as P

HIGH = lax.Precision.HIGHEST


def padded_2(array, sides, width):
    for axis, dim in sides:
        peers, length = (lax.axis_size(axis), array.shape[dim])
        up = [(i, (i + 1) % peers) for i in range(peers - 1)]
        down = [(j, i) for i, j in up]
        last = lax.slice_in_dim(array, length - width, length, axis=dim)
        first = lax.slice_in_dim(array, 0, width, axis=dim)
        before = lax.ppermute(last, axis, up)
        after = lax.ppermute(first, axis, down)
        array = jnp.concatenate([before, array, after], axis=dim)
    return array


def lap_core(padded):
    centre = padded[:, 1:-1, 1:-1, 1:-1]
    summed = padded[:, 2:, 1:-1, 1:-1] + padded[:, :-2, 1:-1, 1:-1]
    summed = summed + padded[:, 1:-1, 2:, 1:-1] + padded[:, 1:-1, :-2, 1:-1]
    summed = summed + padded[:, 1:-1, 1:-1, 2:] + padded[:, 1:-1, 1:-1, :-2]
    return summed - 6.0 * centre


def reaction(centre, coeffs):
    diffusion, prefactor, activation, mixing = coeffs
    temper = 1.5 + jnp.tanh(centre[0])
    rate_terms = (
        prefactor[:, None, None, None]
        * jnp.exp(-activation[:, None, None, None] / temper[None])
        * centre
    )
    return jnp.einsum("vw,wxyz->vxyz", mixing, rate_terms, precision=HIGH)


def tendency(rimmed, centre, coeffs):
    padded = jnp.pad(rimmed, ((0, 0), (0, 0), (0, 0), (1, 1)))
    return coeffs[0][:, None, None, None] * lap_core(padded) + reaction(centre, coeffs)


def inside_mask(rows_x, rows_y):
    pos_x = lax.axis_index("gx") * rows_x + jnp.arange(rows_x + 2) - 1
    pos_y = lax.axis_index("gy") * rows_y + jnp.arange(rows_y + 2) - 1
    in_x = (pos_x >= 0) & (pos_x < rows_x * lax.axis_size("gx"))
    in_y = (pos_y >= 0) & (pos_y < rows_y * lax.axis_size("gy"))
    return in_x[:, None] & in_y[None, :]


def step_deep(state, coeffs, inside):
    wide = padded_2(state, (("gy", 2), ("gx", 1)), 2)
    centre = wide[:, 1:-1, 1:-1]
    section_wide = centre + tendency(wide, centre, coeffs)
    section_wide = jnp.where(inside[None, :, :, None], section_wide, 0.0)
    section = section_wide[:, 1:-1, 1:-1]
    return 0.5 * (state + section + tendency(section_wide, section, coeffs))


def project_y(decoded, basis_y):
    if basis_y.shape[0] * lax.axis_size("gy") == basis_y.shape[1]:
        return decoded
    core = jnp.einsum("xyk,yb->xbk", decoded, basis_y, precision=HIGH)
    return jnp.einsum("xbk,yb->xyk", lax.psum(core, "gy"), basis_y, precision=HIGH)


def mix_x(packed, basis_x):
    rows_x, rows_y, width = packed.shape
    flat = packed.reshape(rows_x, rows_y * width)
    flat = jnp.concatenate([flat, basis_x], axis=1)
    every = lax.all_gather(flat, "gx", axis=0, tiled=True)
    values, basis = every[:, : rows_y * width], every[:, rows_y * width :]
    mixer = jnp.einsum("xa,ua->xu", basis_x, basis, precision=HIGH)
    mixed = jnp.einsum("xu,uk->xk", mixer, values, precision=HIGH)
    return mixed.reshape(rows_x, rows_y, width)


def sum_everywhere(vector):
    axes = ("gx", "gy")
    peers = lax.axis_size(axes)
    if peers > 64:
        return lax.psum(vector, axes)
    sent = jnp.broadcast_to(vector[None], (peers,) + vector.shape)
    return jnp.sum(lax.all_to_all(sent, axes, 0, 0, tiled=True), axis=0)


def on_device(field, diffusion, prefactor, activation, mixing, basis_x, basis_y, basis_z, basis_v):
    coeffs = (diffusion, prefactor, activation, mixing)
    rows_x = field.shape[1]
    rows_y = field.shape[2]
    inside = inside_mask(rows_x, rows_y)
    state = step_deep(field, coeffs, inside)
    rank_z = basis_z.shape[1]
    rank_v = basis_v.shape[1]
    width = rank_z * rank_v
    proj_z = jnp.einsum("vxyz,zr->vxyr", state, basis_z, precision=HIGH)
    packed = jnp.einsum("vxyr,vs->xyrs", proj_z, basis_v, precision=HIGH)
    packed = packed.reshape(rows_x, rows_y, width)
    decoded = project_y(mix_x(packed, basis_x), basis_y)
    decoded = decoded.reshape(rows_x, rows_y, rank_z, rank_v)
    back_v = jnp.einsum("xyrs,vs->vxyr", decoded, basis_v, precision=HIGH)
    recon = jnp.einsum("vxyr,zr->vxyz", back_v, basis_z, precision=HIGH)
    error = state - recon
    miss_local = jnp.sum(error * error, axis=(1, 2, 3))
    mass_local = jnp.sum(state * state, axis=(1, 2, 3))
    sums = sum_everywhere(jnp.concatenate([miss_local, mass_local]))
    miss, mass = jnp.split(sums, 2)
    residual = jnp.sqrt(miss / (mass + 1e-06))
    return (state, recon, residual)


def solution(mesh):
    return jax.shard_map(
        on_device,
        mesh=mesh,
        in_specs=(
            P(None, "gx", "gy", None),
            P(),
            P(),
            P(),
            P(),
            P("gx", None),
            P("gy", None),
            P(),
            P(),
        ),
        out_specs=(P(None, "gx", "gy", None), P(None, "gx", "gy", None), P()),
        check_vma=False,
    )
```

```python
import functools

import jax
import jax.numpy as jnp
from jax import lax
from jax.experimental import pallas as pl
from jax.experimental.pallas import tpu as pltpu
from jax.sharding import PartitionSpec as P

HIGH = lax.Precision.HIGHEST
VM = pl.BlockSpec(memory_space=pltpu.VMEM)
SM = pl.BlockSpec(memory_space=pltpu.SMEM)


def call(kernel, outs, in_specs, name, scratch=(), flops=10**7):
    return pl.pallas_call(
        kernel,
        out_shape=[jax.ShapeDtypeStruct(s, d) for s, d in outs],
        in_specs=in_specs,
        out_specs=[VM] * len(outs),
        scratch_shapes=list(scratch),
        name=name,
        cost_estimate=pl.CostEstimate(flops=flops, bytes_accessed=10**6, transcendentals=0),
    )


def split(a):
    hi = a.astype(jnp.bfloat16)
    lo = (a - hi.astype(jnp.float32)).astype(jnp.bfloat16)
    return hi, lo


def mm(a, b, nt=False):
    dims = (((1,), (1 if nt else 0,)), ((), ()))
    return lax.dot_general(a, b, dims, preferred_element_type=jnp.float32)


def mm3(a, b, nt=False):
    return mm(a[0], b[0], nt) + mm(a[0], b[1], nt) + mm(a[1], b[0], nt)


def place(shape, dim):
    return lax.broadcasted_iota(jnp.int32, shape, dim)


def shifted(w, axis, before=0.0, after=0.0):
    size = w.shape[axis]
    pos = place(w.shape, axis)
    low = jnp.where(pos == 0, before, pltpu.roll(w, 1, axis))
    high = jnp.where(pos == size - 1, after, pltpu.roll(w, size - 1, axis))
    return low + high


def reaction(ws, pre, act, mix):
    n = len(ws)
    cold = -1.0 / (1.5 + jnp.tanh(ws[0]))
    rates = [pre[v] * jnp.exp(act[v] * cold) * ws[v] for v in range(n)]
    outs = []
    for v in range(n):
        total = mix[v, 0] * rates[0]
        for u in range(1, n):
            total = total + mix[v, u] * rates[u]
        outs.append(total)
    return outs


def stage(ref, base_of, nv, rows_x, rows_y, coeffs, emit, low_edge=None, high_edge=None, step=4):
    dif, pre, act, mix = coeffs
    lanes = ref.shape[1]

    def rows(v, x, n):
        return ref[pl.ds(base_of(v, x), n * rows_y), :].reshape(n, rows_y, lanes)

    step = min(step, rows_x)
    for x in range(0, rows_x, step):
        ws = [rows(v, x, step) for v in range(nv)]
        made = reaction(ws, pre, act, mix)
        for v in range(nv):
            w = ws[v]
            if x > 0:
                first = rows(v, x - 1, 1)
            else:
                first = low_edge(v) if low_edge else jnp.zeros((1, rows_y, lanes), jnp.float32)
            if x + step < rows_x:
                last = rows(v, x + step, 1)
            else:
                last = high_edge(v) if high_edge else jnp.zeros((1, rows_y, lanes), jnp.float32)
            if step > 1:
                beside = jnp.concatenate([first, w[:-1]], 0) + jnp.concatenate([w[1:], last], 0)
            else:
                beside = first + last
            lap = beside + shifted(w, 1) + shifted(w, 2) - 6.0 * w
            emit(v, x, step, w, dif[v] * lap + made[v])


def pack_kernel(dims, f_ref, p1, p2, q1, q2):
    nv, rows_x, rows_y, lanes = dims
    odd_x = lax.axis_index("gx") % 2 == 1
    odd_y = lax.axis_index("gy") % 2 == 1
    size = rows_x * rows_y
    for layer in range(2):
        for v in range(nv):
            low = f_ref[pl.ds(v * size + layer, rows_x, stride=rows_y), :]
            high = f_ref[pl.ds(v * size + rows_y - 1 - layer, rows_x, stride=rows_y), :]
            at = pl.ds((layer * nv + v) * rows_x, rows_x)
            p1[at, :] = jnp.where(odd_y, low, high)
            p2[at, :] = jnp.where(odd_y, high, low)
            low = f_ref[pl.ds(v * size + layer * rows_y, rows_y), :]
            high = f_ref[pl.ds(v * size + (rows_x - 1 - layer) * rows_y, rows_y), :]
            at = pl.ds((layer * nv + v) * rows_y, rows_y)
            q1[at, :] = jnp.where(odd_x, low, high)
            q2[at, :] = jnp.where(odd_x, high, low)


def corner_kernel(dims, x1, x2, c1, c2):
    nv, rows_x, rows_y, lanes = dims
    odd_x = lax.axis_index("gx") % 2 == 1
    odd_y = lax.axis_index("gy") % 2 == 1
    for side in range(2):
        for out, swap in ((c1, False), (c2, True)):
            a_low = x1[pl.ds(0, nv, stride=rows_y), :]
            a_high = x1[pl.ds(rows_y - 1, nv, stride=rows_y), :]
            b_low = x2[pl.ds(0, nv, stride=rows_y), :]
            b_high = x2[pl.ds(rows_y - 1, nv, stride=rows_y), :]
            take_one = odd_x if side == 0 else jnp.logical_not(odd_x)
            low = jnp.where(take_one, a_low, b_low)
            high = jnp.where(take_one, a_high, b_high)
            send_low = jnp.logical_not(odd_y) if swap else odd_y
            out[pl.ds(side * nv, nv), :] = jnp.where(send_low, low, high)


def first_kernel(dims, f_ref, bz_ref, bv_ref, dif, pre, act, mix, s_ref, kh, kl, th, tl):
    nv, rows_x, rows_y, lanes = dims
    size = rows_x * rows_y

    def emit(v, x, n, w, t):
        s_ref[pl.ds(v * size + x * rows_y, n * rows_y), :] = (w + t).reshape(n * rows_y, lanes)

    stage(f_ref, lambda v, x: v * size + x * rows_y, nv, rows_x, rows_y, (dif, pre, act, mix), emit)
    bz, bv = bz_ref[...], bv_ref[...]
    rank_z, rank_v = bz.shape[1], bv.shape[1]
    width = rank_z * rank_v
    pick_z = (place((rank_z, width), 1) % rank_z == place((rank_z, width), 0)).astype(jnp.float32)
    pick_v = (place((rank_v, width), 1) // rank_z == place((rank_v, width), 0)).astype(jnp.float32)
    wide_z = jnp.dot(bz, pick_z, precision=HIGH, preferred_element_type=jnp.float32)
    wide_v = jnp.dot(bv, pick_v, precision=HIGH, preferred_element_type=jnp.float32)
    for v in range(nv):
        both = wide_z * wide_v[v : v + 1, :]
        kh[pl.ds(v * lanes, lanes), :], kl[pl.ds(v * lanes, lanes), :] = split(both)
        turned = both.T
        th[:, v * lanes : (v + 1) * lanes], tl[:, v * lanes : (v + 1) * lanes] = split(turned)


def second_kernel(
    dims, f_ref, s_ref, y1, y2, x1, x2, c1, c2, bx_ref, kh, kl, dif, pre, act, mix,
    state_ref, m_ref, sec, gy_ref, gx_ref,
):
    nv, rows_x, rows_y, lanes = dims
    size = rows_x * rows_y
    ix, iy = lax.axis_index("gx"), lax.axis_index("gy")
    odd_x, odd_y = ix % 2 == 1, iy % 2 == 1
    has_x = (ix > 0, ix < lax.axis_size("gx") - 1)
    has_y = (iy > 0, iy < lax.axis_size("gy") - 1)

    def two(one, other, odd, at):
        a, b = one[at, :], other[at, :]
        return jnp.where(odd, a, b), jnp.where(odd, b, a)

    def y_ghost(layer, v):
        return two(y1, y2, odd_y, pl.ds((layer * nv + v) * rows_x, rows_x))

    def x_ghost(layer, v):
        return two(x1, x2, odd_x, pl.ds((layer * nv + v) * rows_y, rows_y))

    def corner(side, v):
        return two(c1, c2, odd_y, pl.ds(side * nv + v, 1))

    def keep(value, flags):
        side = place(value.shape, 0)
        inside = jnp.where(side == 0, flags[0].astype(jnp.int32), flags[1].astype(jnp.int32))
        return jnp.where(inside == 1, value, 0.0)

    gs = [jnp.stack(y_ghost(0, v)) for v in range(nv)]
    made = reaction(gs, pre, act, mix)
    for v in range(nv):
        g = gs[v]
        low = f_ref[pl.ds(v * size, rows_x, stride=rows_y), :]
        high = f_ref[pl.ds(v * size + rows_y - 1, rows_x, stride=rows_y), :]
        before = jnp.stack(corner(0, v))
        after = jnp.stack(corner(1, v))
        lap = jnp.stack(y_ghost(1, v)) + jnp.stack([low, high])
        lap = lap + shifted(g, 1, before, after) + shifted(g, 2) - 6.0 * g
        out = keep(g + (dif[v] * lap + made[v]), has_y)
        gy_ref[pl.ds(v * 2 * rows_x, 2 * rows_x), :] = out.reshape(2 * rows_x, lanes)
        sec[pl.ds(v * size, size), :] = s_ref[pl.ds(v * size, size), :]
        at = pl.ds(v * size, rows_x, stride=rows_y)
        sec[at, :] = sec[at, :] + dif[v] * g[0]
        at = pl.ds(v * size + rows_y - 1, rows_x, stride=rows_y)
        sec[at, :] = sec[at, :] + dif[v] * g[1]
    gs = [jnp.stack(x_ghost(0, v)) for v in range(nv)]
    made = reaction(gs, pre, act, mix)
    for v in range(nv):
        g = gs[v]
        low = f_ref[pl.ds(v * size, rows_y), :]
        high = f_ref[pl.ds(v * size + size - rows_y, rows_y), :]
        left, right = corner(0, v), corner(1, v)
        before = jnp.stack([left[0], right[0]])
        after = jnp.stack([left[1], right[1]])
        lap = jnp.stack(x_ghost(1, v)) + jnp.stack([low, high])
        lap = lap + shifted(g, 1, before, after) + shifted(g, 2) - 6.0 * g
        out = keep(g + (dif[v] * lap + made[v]), has_x)
        gx_ref[pl.ds(v * 2 * rows_y, 2 * rows_y), :] = out.reshape(2 * rows_y, lanes)
        at = pl.ds(v * size, rows_y)
        sec[at, :] = sec[at, :] + dif[v] * g[0]
        at = pl.ds(v * size + size - rows_y, rows_y)
        sec[at, :] = sec[at, :] + dif[v] * g[1]

    def emit(v, x, n, w, t):
        at = pl.ds(v * size + x * rows_y, n * rows_y)
        state_ref[at, :] = 0.5 * ((f_ref[at, :] + w.reshape(n * rows_y, lanes)) + t.reshape(n * rows_y, lanes))

    stage(
        sec, lambda v, x: v * size + x * rows_y, nv, rows_x, rows_y, (dif, pre, act, mix), emit,
        lambda v: gx_ref[pl.ds(v * 2 * rows_y, rows_y), :][None],
        lambda v: gx_ref[pl.ds((v * 2 + 1) * rows_y, rows_y), :][None],
    )
    total = None
    for v in range(nv):
        half = 0.5 * dif[v]
        at = pl.ds(v * size, rows_x, stride=rows_y)
        state_ref[at, :] = state_ref[at, :] + half * gy_ref[pl.ds(v * 2 * rows_x, rows_x), :]
        at = pl.ds(v * size + rows_y - 1, rows_x, stride=rows_y)
        state_ref[at, :] = state_ref[at, :] + half * gy_ref[pl.ds((v * 2 + 1) * rows_x, rows_x), :]
        at = pl.ds(v * lanes, lanes)
        part = mm3(split(state_ref[pl.ds(v * size, size), :]), (kh[at, :], kl[at, :]))
        total = part if total is None else total + part
    bx = bx_ref[...]
    repeated = jnp.broadcast_to(bx[:, None, :], (rows_x, rows_y, bx.shape[1])).reshape(size, bx.shape[1])
    m_ref[...] = jnp.concatenate([total, repeated], axis=1)


def mix_blocks(rows_y, width, blocks):
    own = blocks[0][:, width:]
    size = own.shape[0]
    same = place((size, size), 0) % rows_y == place((size, size), 1) % rows_y
    total = None
    for block in blocks:
        link = lax.dot_general(
            own, block[:, width:], (((1,), (1,)), ((), ())), precision=HIGH, preferred_element_type=jnp.float32
        )
        part = mm3(split(jnp.where(same, link, 0.0)), split(block[:, :width]))
        total = part if total is None else total + part
    return total


def decode_into(decoded, state_ref, th, tl, mass_ref, recon_ref, sums_ref, nv, size, lanes):
    halves = split(decoded)
    sums = mass_ref[...]
    spot = place(sums.shape, 1)
    for v in range(nv):
        cols = slice(v * lanes, (v + 1) * lanes)
        recon = mm3(halves, (th[:, cols], tl[:, cols]))
        at = pl.ds(v * size, size)
        recon_ref[at, :] = recon
        error = state_ref[at, :] - recon
        sums = jnp.where(spot == v, jnp.sum(error * error), sums)
    sums_ref[...] = jnp.broadcast_to(sums, sums_ref.shape)


def third_kernel(dims, width, n, *refs):
    nv, rows_x, rows_y, lanes = dims
    blocks = [ref[...] for ref in refs[:n]]
    state_ref, th, tl, mass_ref, recon_ref, sums_ref = refs[n:]
    decoded = mix_blocks(rows_y, width, blocks)
    decode_into(decoded, state_ref, th, tl, mass_ref, recon_ref, sums_ref, nv, rows_x * rows_y, lanes)


def mix_kernel(rows_y, width, n, *refs):
    refs[n][...] = mix_blocks(rows_y, width, [ref[...] for ref in refs[:n]])


def decode_kernel(dims, d_ref, state_ref, th, tl, mass_ref, recon_ref, sums_ref):
    nv, rows_x, rows_y, lanes = dims
    decode_into(d_ref[...], state_ref, th, tl, mass_ref, recon_ref, sums_ref, nv, rows_x * rows_y, lanes)


def mass_kernel(dims, state_ref, out_ref):
    nv, rows_x, rows_y, lanes = dims
    size = rows_x * rows_y
    spot = place(out_ref.shape, 1)
    sums = jnp.zeros(out_ref.shape, jnp.float32)
    for v in range(nv):
        w = state_ref[pl.ds(v * size, size), :]
        sums = jnp.where(spot == nv + v, jnp.sum(w * w), sums)
    out_ref[...] = sums


def pairs(n, first):
    swaps = [(i, i + 1) for i in range(first, n - 1, 2)]
    return swaps + [(j, i) for i, j in swaps]


def gather_blocks(block):
    n = lax.axis_size("gx")
    if n & (n - 1):
        every = lax.all_gather(block, "gx", axis=0)
        return [block] + [jnp.roll(every, -lax.axis_index("gx"), 0)[i] for i in range(1, n)]
    blocks = [block]
    bit = n // 2
    while bit:
        swaps = [(i, i ^ bit) for i in range(n)]
        blocks = blocks + [lax.ppermute(b, "gx", swaps) for b in blocks]
        bit //= 2
    return blocks


def on_device(field, diffusion, prefactor, activation, mixing, basis_x, basis_y, basis_z, basis_v):
    f32, bf16 = jnp.float32, jnp.bfloat16
    dims = field.shape
    nv, rows_x, rows_y, lanes = dims
    size = rows_x * rows_y
    rank_z, rank_v = basis_z.shape[1], basis_v.shape[1]
    width = rank_z * rank_v
    gx, gy = lax.axis_size("gx"), lax.axis_size("gy")
    peers = gx * gy
    coeffs = (diffusion, prefactor, activation, mixing)
    flat = field.reshape(nv * size, lanes)

    y_msg, x_msg = (2 * nv * rows_x, lanes), (2 * nv * rows_y, lanes)
    p1, p2, q1, q2 = call(
        functools.partial(pack_kernel, dims), [(y_msg, f32)] * 2 + [(x_msg, f32)] * 2, [VM], "pack"
    )(flat)
    y1 = lax.ppermute(p1, "gy", pairs(gy, 0))
    y2 = lax.ppermute(p2, "gy", pairs(gy, 1))
    x1 = lax.ppermute(q1, "gx", pairs(gx, 0))
    x2 = lax.ppermute(q2, "gx", pairs(gx, 1))
    c1, c2 = call(
        functools.partial(corner_kernel, dims), [((2 * nv, lanes), f32)] * 2, [VM] * 2, "corner"
    )(x1, x2)
    c1 = lax.ppermute(c1, "gy", pairs(gy, 0))
    c2 = lax.ppermute(c2, "gy", pairs(gy, 1))

    section, kh, kl, th, tl = call(
        functools.partial(first_kernel, dims),
        [((nv * size, lanes), f32)] + [((nv * lanes, width), bf16)] * 2 + [((width, nv * lanes), bf16)] * 2,
        [VM] * 3 + [SM] * 4,
        "first",
    )(flat, basis_z, basis_v, *coeffs)
    state, message = call(
        functools.partial(second_kernel, dims),
        [((nv * size, lanes), f32), ((size, width + basis_x.shape[1]), f32)],
        [VM] * 11 + [SM] * 4,
        "second",
        [
            pltpu.VMEM((nv * size, lanes), f32),
            pltpu.VMEM((nv * 2 * rows_x, lanes), f32),
            pltpu.VMEM((nv * 2 * rows_y, lanes), f32),
        ],
    )(flat, section, y1, y2, x1, x2, c1, c2, basis_x, kh, kl, *coeffs)
    blocks = gather_blocks(message)
    (mass_row,) = call(functools.partial(mass_kernel, dims), [((1, lanes), f32)], [VM], "mass")(state)
    outs = [((nv * size, lanes), f32), ((peers, lanes), f32)]
    if basis_y.shape[0] * gy == basis_y.shape[1]:
        recon, sums = call(
            functools.partial(third_kernel, dims, width, len(blocks)), outs, [VM] * (len(blocks) + 4), "third"
        )(*blocks, state, th, tl, mass_row)
    else:
        (mixed,) = call(
            functools.partial(mix_kernel, rows_y, width, len(blocks)), [((size, width), f32)], [VM] * len(blocks), "mixed"
        )(*blocks)
        mixed = mixed.reshape(rows_x, rows_y, width)
        core = lax.psum(jnp.einsum("xyk,yb->xbk", mixed, basis_y, precision=HIGH), "gy")
        mixed = jnp.einsum("xbk,yb->xyk", core, basis_y, precision=HIGH).reshape(size, width)
        recon, sums = call(functools.partial(decode_kernel, dims), outs, [VM] * 5, "decode")(
            mixed, state, th, tl, mass_row
        )
    if peers > 64:
        sums = lax.psum(sums[0], ("gx", "gy"))
    else:
        sums = jnp.sum(lax.all_to_all(sums, ("gx", "gy"), 0, 0, tiled=True), axis=0)
    residual = jnp.sqrt(sums[:nv] / (sums[nv : 2 * nv] + 1e-06))
    return (state.reshape(dims), recon.reshape(dims), residual)


def solution(mesh):
    return jax.shard_map(
        on_device,
        mesh=mesh,
        in_specs=(
            P(None, "gx", "gy", None),
            P(),
            P(),
            P(),
            P(),
            P("gx", None),
            P("gy", None),
            P(),
            P(),
        ),
        out_specs=(P(None, "gx", "gy", None), P(None, "gx", "gy", None), P()),
        check_vma=False,
    )
```

```python
import functools

import jax
import jax.numpy as jnp
from jax import lax
from jax.experimental import pallas as pl
from jax.experimental.pallas import tpu as pltpu
from jax.sharding import PartitionSpec as P

HIGH = lax.Precision.HIGHEST
VM = pl.BlockSpec(memory_space=pltpu.VMEM)
SM = pl.BlockSpec(memory_space=pltpu.SMEM)


def call(kernel, outs, in_specs, name, scratch=(), flops=10**7, vmem=12):
    return pl.pallas_call(
        kernel,
        out_shape=[jax.ShapeDtypeStruct(s, d) for s, d in outs],
        in_specs=in_specs,
        out_specs=[VM] * len(outs),
        scratch_shapes=list(scratch),
        name=name,
        compiler_params=pltpu.CompilerParams(vmem_limit_bytes=vmem << 20),
        cost_estimate=pl.CostEstimate(flops=flops, bytes_accessed=10**6, transcendentals=0),
    )


def split(a):
    hi = a.astype(jnp.bfloat16)
    lo = (a - hi.astype(jnp.float32)).astype(jnp.bfloat16)
    return hi, lo


def mm(a, b, nt=False):
    dims = (((1,), (1 if nt else 0,)), ((), ()))
    return lax.dot_general(a, b, dims, preferred_element_type=jnp.float32)


def mm3(a, b, nt=False):
    return mm(a[0], b[0], nt) + mm(a[0], b[1], nt) + mm(a[1], b[0], nt)


def place(shape, dim):
    return lax.broadcasted_iota(jnp.int32, shape, dim)


def shifted(w, axis, before=0.0, after=0.0):
    size = w.shape[axis]
    pos = place(w.shape, axis)
    low = jnp.where(pos == 0, before, pltpu.roll(w, 1, axis))
    high = jnp.where(pos == size - 1, after, pltpu.roll(w, size - 1, axis))
    return low + high


def reaction(ws, pre, act, mix):
    n = len(ws)
    cold = -1.0 / (1.5 + jnp.tanh(ws[0]))
    rates = [pre[v] * jnp.exp(act[v] * cold) * ws[v] for v in range(n)]
    outs = []
    for v in range(n):
        total = mix[v, 0] * rates[0]
        for u in range(1, n):
            total = total + mix[v, u] * rates[u]
        outs.append(total)
    return outs


def stage(ref, base_of, nv, rows_x, rows_y, coeffs, emit, low_edge=None, high_edge=None, step=4):
    dif, pre, act, mix = coeffs
    lanes = ref.shape[1]

    def rows(v, x, n):
        return ref[pl.ds(base_of(v, x), n * rows_y), :].reshape(n, rows_y, lanes)

    step = min(step, rows_x)
    for x in range(0, rows_x, step):
        ws = [rows(v, x, step) for v in range(nv)]
        made = reaction(ws, pre, act, mix)
        for v in range(nv):
            w = ws[v]
            if x > 0:
                first = rows(v, x - 1, 1)
            else:
                first = low_edge(v) if low_edge else jnp.zeros((1, rows_y, lanes), jnp.float32)
            if x + step < rows_x:
                last = rows(v, x + step, 1)
            else:
                last = high_edge(v) if high_edge else jnp.zeros((1, rows_y, lanes), jnp.float32)
            if step > 1:
                beside = jnp.concatenate([first, w[:-1]], 0) + jnp.concatenate([w[1:], last], 0)
            else:
                beside = first + last
            lap = beside + shifted(w, 1) + shifted(w, 2) - 6.0 * w
            emit(v, x, step, w, dif[v] * lap + made[v])


def pack_kernel(dims, f_ref, p1, p2, q1, q2):
    nv, rows_x, rows_y, lanes = dims
    odd_x = lax.axis_index("gx") % 2 == 1
    odd_y = lax.axis_index("gy") % 2 == 1
    size = rows_x * rows_y
    for layer in range(2):
        for v in range(nv):
            low = f_ref[pl.ds(v * size + layer, rows_x, stride=rows_y), :]
            high = f_ref[pl.ds(v * size + rows_y - 1 - layer, rows_x, stride=rows_y), :]
            at = pl.ds((layer * nv + v) * rows_x, rows_x)
            p1[at, :] = jnp.where(odd_y, low, high)
            p2[at, :] = jnp.where(odd_y, high, low)
            low = f_ref[pl.ds(v * size + layer * rows_y, rows_y), :]
            high = f_ref[pl.ds(v * size + (rows_x - 1 - layer) * rows_y, rows_y), :]
            at = pl.ds((layer * nv + v) * rows_y, rows_y)
            q1[at, :] = jnp.where(odd_x, low, high)
            q2[at, :] = jnp.where(odd_x, high, low)


def corner_kernel(dims, x1, x2, c1, c2):
    nv, rows_x, rows_y, lanes = dims
    odd_x = lax.axis_index("gx") % 2 == 1
    odd_y = lax.axis_index("gy") % 2 == 1
    for side in range(2):
        for out, swap in ((c1, False), (c2, True)):
            a_low = x1[pl.ds(0, nv, stride=rows_y), :]
            a_high = x1[pl.ds(rows_y - 1, nv, stride=rows_y), :]
            b_low = x2[pl.ds(0, nv, stride=rows_y), :]
            b_high = x2[pl.ds(rows_y - 1, nv, stride=rows_y), :]
            take_one = odd_x if side == 0 else jnp.logical_not(odd_x)
            low = jnp.where(take_one, a_low, b_low)
            high = jnp.where(take_one, a_high, b_high)
            send_low = jnp.logical_not(odd_y) if swap else odd_y
            out[pl.ds(side * nv, nv), :] = jnp.where(send_low, low, high)


def first_kernel(dims, f_ref, bz_ref, bv_ref, dif, pre, act, mix, s_ref, kh, kl, th, tl):
    nv, rows_x, rows_y, lanes = dims
    size = rows_x * rows_y

    def emit(v, x, n, w, t):
        s_ref[pl.ds(v * size + x * rows_y, n * rows_y), :] = (w + t).reshape(n * rows_y, lanes)

    stage(f_ref, lambda v, x: v * size + x * rows_y, nv, rows_x, rows_y, (dif, pre, act, mix), emit)
    bz, bv = bz_ref[...], bv_ref[...]
    rank_z, rank_v = bz.shape[0], bv.shape[0]
    width = rank_z * rank_v
    pick_z = (place((rank_z, width), 1) % rank_z == place((rank_z, width), 0)).astype(jnp.float32)
    pick_v = (place((rank_v, width), 1) // rank_z == place((rank_v, width), 0)).astype(jnp.float32)
    first = (((0,), (0,)), ((), ()))
    wide_z = lax.dot_general(bz, pick_z, first, precision=HIGH, preferred_element_type=jnp.float32)
    wide_v = lax.dot_general(bv, pick_v, first, precision=HIGH, preferred_element_type=jnp.float32)
    for v in range(nv):
        both = wide_z * wide_v[v : v + 1, :]
        kh[pl.ds(v * lanes, lanes), :], kl[pl.ds(v * lanes, lanes), :] = split(both)
        turned = both.T
        th[:, v * lanes : (v + 1) * lanes], tl[:, v * lanes : (v + 1) * lanes] = split(turned)


def second_kernel(
    dims, f_ref, s_ref, y1, y2, x1, x2, c1, c2, bx_ref, kh, kl, dif, pre, act, mix,
    state_ref, m_ref, sec, gy_ref, gx_ref,
):
    nv, rows_x, rows_y, lanes = dims
    size = rows_x * rows_y
    ix, iy = lax.axis_index("gx"), lax.axis_index("gy")
    odd_x, odd_y = ix % 2 == 1, iy % 2 == 1
    has_x = (ix > 0, ix < lax.axis_size("gx") - 1)
    has_y = (iy > 0, iy < lax.axis_size("gy") - 1)

    def two(one, other, odd, at):
        a, b = one[at, :], other[at, :]
        return jnp.where(odd, a, b), jnp.where(odd, b, a)

    def y_ghost(layer, v):
        return two(y1, y2, odd_y, pl.ds((layer * nv + v) * rows_x, rows_x))

    def x_ghost(layer, v):
        return two(x1, x2, odd_x, pl.ds((layer * nv + v) * rows_y, rows_y))

    def corner(side, v):
        return two(c1, c2, odd_y, pl.ds(side * nv + v, 1))

    def keep(value, flags):
        side = place(value.shape, 0)
        inside = jnp.where(side == 0, flags[0].astype(jnp.int32), flags[1].astype(jnp.int32))
        return jnp.where(inside == 1, value, 0.0)

    gs = [jnp.stack(y_ghost(0, v)) for v in range(nv)]
    made = reaction(gs, pre, act, mix)
    for v in range(nv):
        g = gs[v]
        low = f_ref[pl.ds(v * size, rows_x, stride=rows_y), :]
        high = f_ref[pl.ds(v * size + rows_y - 1, rows_x, stride=rows_y), :]
        before = jnp.stack(corner(0, v))
        after = jnp.stack(corner(1, v))
        lap = jnp.stack(y_ghost(1, v)) + jnp.stack([low, high])
        lap = lap + shifted(g, 1, before, after) + shifted(g, 2) - 6.0 * g
        out = keep(g + (dif[v] * lap + made[v]), has_y)
        gy_ref[pl.ds(v * 2 * rows_x, 2 * rows_x), :] = out.reshape(2 * rows_x, lanes)
        sec[pl.ds(v * size, size), :] = s_ref[pl.ds(v * size, size), :]
        at = pl.ds(v * size, rows_x, stride=rows_y)
        sec[at, :] = sec[at, :] + dif[v] * g[0]
        at = pl.ds(v * size + rows_y - 1, rows_x, stride=rows_y)
        sec[at, :] = sec[at, :] + dif[v] * g[1]
    gs = [jnp.stack(x_ghost(0, v)) for v in range(nv)]
    made = reaction(gs, pre, act, mix)
    for v in range(nv):
        g = gs[v]
        low = f_ref[pl.ds(v * size, rows_y), :]
        high = f_ref[pl.ds(v * size + size - rows_y, rows_y), :]
        left, right = corner(0, v), corner(1, v)
        before = jnp.stack([left[0], right[0]])
        after = jnp.stack([left[1], right[1]])
        lap = jnp.stack(x_ghost(1, v)) + jnp.stack([low, high])
        lap = lap + shifted(g, 1, before, after) + shifted(g, 2) - 6.0 * g
        out = keep(g + (dif[v] * lap + made[v]), has_x)
        gx_ref[pl.ds(v * 2 * rows_y, 2 * rows_y), :] = out.reshape(2 * rows_y, lanes)
        at = pl.ds(v * size, rows_y)
        sec[at, :] = sec[at, :] + dif[v] * g[0]
        at = pl.ds(v * size + size - rows_y, rows_y)
        sec[at, :] = sec[at, :] + dif[v] * g[1]

    def emit(v, x, n, w, t):
        at = pl.ds(v * size + x * rows_y, n * rows_y)
        state_ref[at, :] = 0.5 * ((f_ref[at, :] + w.reshape(n * rows_y, lanes)) + t.reshape(n * rows_y, lanes))

    stage(
        sec, lambda v, x: v * size + x * rows_y, nv, rows_x, rows_y, (dif, pre, act, mix), emit,
        lambda v: gx_ref[pl.ds(v * 2 * rows_y, rows_y), :][None],
        lambda v: gx_ref[pl.ds((v * 2 + 1) * rows_y, rows_y), :][None],
    )
    total = None
    for v in range(nv):
        half = 0.5 * dif[v]
        at = pl.ds(v * size, rows_x, stride=rows_y)
        state_ref[at, :] = state_ref[at, :] + half * gy_ref[pl.ds(v * 2 * rows_x, rows_x), :]
        at = pl.ds(v * size + rows_y - 1, rows_x, stride=rows_y)
        state_ref[at, :] = state_ref[at, :] + half * gy_ref[pl.ds((v * 2 + 1) * rows_x, rows_x), :]
        at = pl.ds(v * lanes, lanes)
        part = mm3(split(state_ref[pl.ds(v * size, size), :]), (kh[at, :], kl[at, :]))
        total = part if total is None else total + part
    bx = bx_ref[...]
    repeated = jnp.broadcast_to(bx[:, None, :], (rows_x, rows_y, bx.shape[1])).reshape(size, bx.shape[1])
    m_ref[...] = jnp.concatenate([total, repeated], axis=1)


def mix_blocks(rows_y, width, blocks):
    own = blocks[0][:, width:]
    size = own.shape[0]
    same = place((size, size), 0) % rows_y == place((size, size), 1) % rows_y
    total = None
    for block in blocks:
        link = lax.dot_general(
            own, block[:, width:], (((1,), (1,)), ((), ())), precision=HIGH, preferred_element_type=jnp.float32
        )
        part = mm3(split(jnp.where(same, link, 0.0)), split(block[:, :width]))
        total = part if total is None else total + part
    return total


def decode_into(decoded, state_ref, th, tl, mass_ref, recon_ref, sums_ref, nv, size, lanes):
    halves = split(decoded)
    sums = mass_ref[...]
    spot = place(sums.shape, 1)
    for v in range(nv):
        cols = slice(v * lanes, (v + 1) * lanes)
        recon = mm3(halves, (th[:, cols], tl[:, cols]))
        at = pl.ds(v * size, size)
        recon_ref[at, :] = recon
        error = state_ref[at, :] - recon
        sums = jnp.where(spot == v, jnp.sum(error * error), sums)
    sums_ref[...] = jnp.broadcast_to(sums, sums_ref.shape)


def third_kernel(dims, width, n, *refs):
    nv, rows_x, rows_y, lanes = dims
    blocks = [ref[...] for ref in refs[:n]]
    state_ref, th, tl, mass_ref, recon_ref, sums_ref = refs[n:]
    decoded = mix_blocks(rows_y, width, blocks)
    decode_into(decoded, state_ref, th, tl, mass_ref, recon_ref, sums_ref, nv, rows_x * rows_y, lanes)


def mix_kernel(rows_y, width, n, *refs):
    refs[n][...] = mix_blocks(rows_y, width, [ref[...] for ref in refs[:n]])


def decode_kernel(dims, d_ref, state_ref, th, tl, mass_ref, recon_ref, sums_ref):
    nv, rows_x, rows_y, lanes = dims
    decode_into(d_ref[...], state_ref, th, tl, mass_ref, recon_ref, sums_ref, nv, rows_x * rows_y, lanes)


def mass_kernel(dims, state_ref, out_ref):
    nv, rows_x, rows_y, lanes = dims
    size = rows_x * rows_y
    spot = place(out_ref.shape, 1)
    sums = jnp.zeros(out_ref.shape, jnp.float32)
    for v in range(nv):
        w = state_ref[pl.ds(v * size, size), :]
        sums = jnp.where(spot == nv + v, jnp.sum(w * w), sums)
    out_ref[...] = sums


def pairs(n, first):
    swaps = [(i, i + 1) for i in range(first, n - 1, 2)]
    return swaps + [(j, i) for i, j in swaps]


def gather_blocks(block):
    n = lax.axis_size("gx")
    if n & (n - 1):
        every = lax.all_gather(block, "gx", axis=0)
        return [block] + [jnp.roll(every, -lax.axis_index("gx"), 0)[i] for i in range(1, n)]
    blocks = [block]
    bit = n // 2
    while bit:
        swaps = [(i, i ^ bit) for i in range(n)]
        blocks = blocks + [lax.ppermute(b, "gx", swaps) for b in blocks]
        bit //= 2
    return blocks


def on_device(field, diffusion, prefactor, activation, mixing, basis_x, basis_y, basis_z, basis_v):
    f32, bf16 = jnp.float32, jnp.bfloat16
    dims = field.shape
    nv, rows_x, rows_y, lanes = dims
    size = rows_x * rows_y
    rank_z, rank_v = basis_z.shape[1], basis_v.shape[1]
    width = rank_z * rank_v
    gx, gy = lax.axis_size("gx"), lax.axis_size("gy")
    peers = gx * gy
    coeffs = (diffusion, prefactor, activation, mixing)
    flat = field.reshape(nv * size, lanes)

    y_msg, x_msg = (2 * nv * rows_x, lanes), (2 * nv * rows_y, lanes)
    p1, p2, q1, q2 = call(
        functools.partial(pack_kernel, dims), [(y_msg, f32)] * 2 + [(x_msg, f32)] * 2, [VM], "pack"
    )(flat)
    y1 = lax.ppermute(p1, "gy", pairs(gy, 0))
    y2 = lax.ppermute(p2, "gy", pairs(gy, 1))
    x1 = lax.ppermute(q1, "gx", pairs(gx, 0))
    x2 = lax.ppermute(q2, "gx", pairs(gx, 1))
    c1, c2 = call(
        functools.partial(corner_kernel, dims), [((2 * nv, lanes), f32)] * 2, [VM] * 2, "corner"
    )(x1, x2)
    c1 = lax.ppermute(c1, "gy", pairs(gy, 0))
    c2 = lax.ppermute(c2, "gy", pairs(gy, 1))

    section, kh, kl, th, tl = call(
        functools.partial(first_kernel, dims),
        [((nv * size, lanes), f32)] + [((nv * lanes, width), bf16)] * 2 + [((width, nv * lanes), bf16)] * 2,
        [VM] * 3 + [SM] * 4,
        "first",
    )(flat, basis_z.T, basis_v.T, *coeffs)
    state, message = call(
        functools.partial(second_kernel, dims),
        [((nv * size, lanes), f32), ((size, width + basis_x.shape[1]), f32)],
        [VM] * 11 + [SM] * 4,
        "second",
        [
            pltpu.VMEM((nv * size, lanes), f32),
            pltpu.VMEM((nv * 2 * rows_x, lanes), f32),
            pltpu.VMEM((nv * 2 * rows_y, lanes), f32),
        ],
    )(flat, section, y1, y2, x1, x2, c1, c2, basis_x, kh, kl, *coeffs)
    blocks = gather_blocks(message)
    (mass_row,) = call(functools.partial(mass_kernel, dims), [((1, lanes), f32)], [VM], "mass")(state)
    outs = [((nv * size, lanes), f32), ((peers, lanes), f32)]
    if basis_y.shape[0] * gy == basis_y.shape[1]:
        recon, sums = call(
            functools.partial(third_kernel, dims, width, len(blocks)), outs, [VM] * (len(blocks) + 4), "third"
        )(*blocks, state, th, tl, mass_row)
    else:
        (mixed,) = call(
            functools.partial(mix_kernel, rows_y, width, len(blocks)), [((size, width), f32)], [VM] * len(blocks), "mixed"
        )(*blocks)
        mixed = mixed.reshape(rows_x, rows_y, width)
        core = lax.psum(jnp.einsum("xyk,yb->xbk", mixed, basis_y, precision=HIGH), "gy")
        mixed = jnp.einsum("xbk,yb->xyk", core, basis_y, precision=HIGH).reshape(size, width)
        recon, sums = call(functools.partial(decode_kernel, dims), outs, [VM] * 5, "decode")(
            mixed, state, th, tl, mass_row
        )
    if peers > 64:
        sums = lax.psum(sums[0], ("gx", "gy"))
    else:
        sums = jnp.sum(lax.all_to_all(sums, ("gx", "gy"), 0, 0, tiled=True), axis=0)
    residual = jnp.sqrt(sums[:nv] / (sums[nv : 2 * nv] + 1e-06))
    return (state.reshape(dims), recon.reshape(dims), residual)


def solution(mesh):
    return jax.shard_map(
        on_device,
        mesh=mesh,
        in_specs=(
            P(None, "gx", "gy", None),
            P(),
            P(),
            P(),
            P(),
            P("gx", None),
            P("gy", None),
            P(),
            P(),
        ),
        out_specs=(P(None, "gx", "gy", None), P(None, "gx", "gy", None), P()),
        check_vma=False,
    )
```

```python
import functools

import jax
import jax.numpy as jnp
from jax import lax
from jax.experimental import pallas as pl
from jax.experimental.pallas import tpu as pltpu
from jax.sharding import PartitionSpec as P


HIGH = lax.Precision.HIGHEST
VM = pl.BlockSpec(memory_space=pltpu.VMEM)
SM = pl.BlockSpec(memory_space=pltpu.SMEM)


def call(kernel, outs, in_specs, scratch=(), flops=10**7, vmem=12):
    return pl.pallas_call(
        kernel,
        out_shape=[jax.ShapeDtypeStruct(s, d) for s, d in outs],
        in_specs=in_specs,
        out_specs=[VM] * len(outs),
        scratch_shapes=list(scratch),
        compiler_params=pltpu.CompilerParams(vmem_limit_bytes=vmem << 20),
        cost_estimate=pl.CostEstimate(flops=flops, bytes_accessed=10**6, transcendentals=0),
    )


def split(a):
    hi = a.astype(jnp.bfloat16)
    lo = (a - hi.astype(jnp.float32)).astype(jnp.bfloat16)
    return hi, lo


def mm(a, b, nt=False):
    dims = (((1,), (1 if nt else 0,)), ((), ()))
    return lax.dot_general(a, b, dims, preferred_element_type=jnp.float32)


def mm3(a, b, nt=False):
    return mm(a[0], b[0], nt) + mm(a[0], b[1], nt) + mm(a[1], b[0], nt)


def place(shape, dim):
    return lax.broadcasted_iota(jnp.int32, shape, dim)


def shifted(w, axis, before=0.0, after=0.0):
    size = w.shape[axis]
    pos = place(w.shape, axis)
    low = jnp.where(pos == 0, before, pltpu.roll(w, 1, axis))
    high = jnp.where(pos == size - 1, after, pltpu.roll(w, size - 1, axis))
    return low + high


def reaction(ws, pre, act, mix):
    n = len(ws)
    cold = -1.0 / (1.5 + jnp.tanh(ws[0]))
    rates = [pre[v] * jnp.exp(act[v] * cold) * ws[v] for v in range(n)]
    outs = []
    for v in range(n):
        total = mix[v, 0] * rates[0]
        for u in range(1, n):
            total = total + mix[v, u] * rates[u]
        outs.append(total)
    return outs


def stage(ref, base_of, nv, rows_x, rows_y, coeffs, emit, low_edge=None, high_edge=None, step=4):
    dif, pre, act, mix = coeffs
    lanes = ref.shape[1]

    def rows(v, x, n):
        return ref[pl.ds(base_of(v, x), n * rows_y), :].reshape(n, rows_y, lanes)

    step = min(step, rows_x)
    for x in range(0, rows_x, step):
        ws = [rows(v, x, step) for v in range(nv)]
        made = reaction(ws, pre, act, mix)
        for v in range(nv):
            w = ws[v]
            if x > 0:
                first = rows(v, x - 1, 1)
            else:
                first = low_edge(v) if low_edge else jnp.zeros((1, rows_y, lanes), jnp.float32)
            if x + step < rows_x:
                last = rows(v, x + step, 1)
            else:
                last = high_edge(v) if high_edge else jnp.zeros((1, rows_y, lanes), jnp.float32)
            if step > 1:
                beside = jnp.concatenate([first, w[:-1]], 0) + jnp.concatenate([w[1:], last], 0)
            else:
                beside = first + last
            lap = beside + shifted(w, 1) + shifted(w, 2) - 6.0 * w
            emit(v, x, step, w, dif[v] * lap + made[v])


def pack_kernel(dims, f_ref, p1, p2, q1, q2):
    nv, rows_x, rows_y, _ = dims
    odd_x = lax.axis_index("gx") % 2 == 1
    odd_y = lax.axis_index("gy") % 2 == 1
    size = rows_x * rows_y
    for layer in range(2):
        for v in range(nv):
            low = f_ref[pl.ds(v * size + layer, rows_x, stride=rows_y), :]
            high = f_ref[pl.ds(v * size + rows_y - 1 - layer, rows_x, stride=rows_y), :]
            at = pl.ds((layer * nv + v) * rows_x, rows_x)
            p1[at, :] = jnp.where(odd_y, low, high)
            p2[at, :] = jnp.where(odd_y, high, low)
            low = f_ref[pl.ds(v * size + layer * rows_y, rows_y), :]
            high = f_ref[pl.ds(v * size + (rows_x - 1 - layer) * rows_y, rows_y), :]
            at = pl.ds((layer * nv + v) * rows_y, rows_y)
            q1[at, :] = jnp.where(odd_x, low, high)
            q2[at, :] = jnp.where(odd_x, high, low)


def corner_kernel(dims, x1, x2, c1, c2):
    nv, _, rows_y, _ = dims
    odd_x = lax.axis_index("gx") % 2 == 1
    odd_y = lax.axis_index("gy") % 2 == 1
    for side in range(2):
        for out, swap in ((c1, False), (c2, True)):
            a_low = x1[pl.ds(0, nv, stride=rows_y), :]
            a_high = x1[pl.ds(rows_y - 1, nv, stride=rows_y), :]
            b_low = x2[pl.ds(0, nv, stride=rows_y), :]
            b_high = x2[pl.ds(rows_y - 1, nv, stride=rows_y), :]
            take_one = odd_x if side == 0 else jnp.logical_not(odd_x)
            low = jnp.where(take_one, a_low, b_low)
            high = jnp.where(take_one, a_high, b_high)
            send_low = jnp.logical_not(odd_y) if swap else odd_y
            out[pl.ds(side * nv, nv), :] = jnp.where(send_low, low, high)


def first_kernel(dims, f_ref, bz_ref, bv_ref, dif, pre, act, mix, s_ref, kh, kl, th, tl, uh, ul):
    nv, rows_x, rows_y, lanes = dims
    size = rows_x * rows_y

    def emit(v, x, n, w, t):
        s_ref[pl.ds(v * size + x * rows_y, n * rows_y), :] = (w + t).reshape(n * rows_y, lanes)

    stage(f_ref, lambda v, x: v * size + x * rows_y, nv, rows_x, rows_y, (dif, pre, act, mix), emit)
    bz, bv = bz_ref[...], bv_ref[...]
    rank_z, rank_v = bz.shape[0], bv.shape[0]
    width = rank_z * rank_v
    pick_z = (place((rank_z, width), 1) % rank_z == place((rank_z, width), 0)).astype(jnp.float32)
    pick_v = (place((rank_v, width), 1) // rank_z == place((rank_v, width), 0)).astype(jnp.float32)
    first = (((0,), (0,)), ((), ()))
    wide_z = lax.dot_general(bz, pick_z, first, precision=HIGH, preferred_element_type=jnp.float32)
    wide_v = lax.dot_general(bv, pick_v, first, precision=HIGH, preferred_element_type=jnp.float32)
    for v in range(nv):
        both = wide_z * wide_v[v : v + 1, :]
        kh[pl.ds(v * lanes, lanes), :], kl[pl.ds(v * lanes, lanes), :] = split(both)
        turned = both.T
        th[:, v * lanes : (v + 1) * lanes], tl[:, v * lanes : (v + 1) * lanes] = split(turned)
    part = nv * rank_z
    pick_u = (place((nv, part), 1) // rank_z == place((nv, part), 0)).astype(jnp.float32)
    tall = lax.dot_general(pick_v, bv, first, precision=HIGH, preferred_element_type=jnp.float32)
    tall = jnp.dot(tall, pick_u, precision=HIGH, preferred_element_type=jnp.float32)
    same = place((width, part), 0) % rank_z == place((width, part), 1) % rank_z
    uh[...], ul[...] = split(jnp.where(same, tall, 0.0))


def second_kernel(
    dims, f_ref, s_ref, y1, y2, x1, x2, c1, c2, bx_ref, kh, kl, dif, pre, act, mix,
    state_ref, m_ref, sec, gy_ref, gx_ref,
):
    nv, rows_x, rows_y, lanes = dims
    size = rows_x * rows_y
    ix, iy = lax.axis_index("gx"), lax.axis_index("gy")
    odd_x, odd_y = ix % 2 == 1, iy % 2 == 1
    has_x = (ix > 0, ix < lax.axis_size("gx") - 1)
    has_y = (iy > 0, iy < lax.axis_size("gy") - 1)

    def two(one, other, odd, at):
        a, b = one[at, :], other[at, :]
        return jnp.where(odd, a, b), jnp.where(odd, b, a)

    def y_ghost(layer, v):
        return two(y1, y2, odd_y, pl.ds((layer * nv + v) * rows_x, rows_x))

    def x_ghost(layer, v):
        return two(x1, x2, odd_x, pl.ds((layer * nv + v) * rows_y, rows_y))

    def corner(side, v):
        return two(c1, c2, odd_y, pl.ds(side * nv + v, 1))

    def keep(value, flags):
        side = place(value.shape, 0)
        inside = jnp.where(side == 0, flags[0].astype(jnp.int32), flags[1].astype(jnp.int32))
        return jnp.where(inside == 1, value, 0.0)

    gs = [jnp.stack(y_ghost(0, v)) for v in range(nv)]
    made = reaction(gs, pre, act, mix)
    for v in range(nv):
        g = gs[v]
        low = f_ref[pl.ds(v * size, rows_x, stride=rows_y), :]
        high = f_ref[pl.ds(v * size + rows_y - 1, rows_x, stride=rows_y), :]
        before = jnp.stack(corner(0, v))
        after = jnp.stack(corner(1, v))
        lap = jnp.stack(y_ghost(1, v)) + jnp.stack([low, high])
        lap = lap + shifted(g, 1, before, after) + shifted(g, 2) - 6.0 * g
        out = keep(g + (dif[v] * lap + made[v]), has_y)
        gy_ref[pl.ds(v * 2 * rows_x, 2 * rows_x), :] = out.reshape(2 * rows_x, lanes)
        sec[pl.ds(v * size, size), :] = s_ref[pl.ds(v * size, size), :]
        at = pl.ds(v * size, rows_x, stride=rows_y)
        sec[at, :] = sec[at, :] + dif[v] * g[0]
        at = pl.ds(v * size + rows_y - 1, rows_x, stride=rows_y)
        sec[at, :] = sec[at, :] + dif[v] * g[1]
    gs = [jnp.stack(x_ghost(0, v)) for v in range(nv)]
    made = reaction(gs, pre, act, mix)
    for v in range(nv):
        g = gs[v]
        low = f_ref[pl.ds(v * size, rows_y), :]
        high = f_ref[pl.ds(v * size + size - rows_y, rows_y), :]
        left, right = corner(0, v), corner(1, v)
        before = jnp.stack([left[0], right[0]])
        after = jnp.stack([left[1], right[1]])
        lap = jnp.stack(x_ghost(1, v)) + jnp.stack([low, high])
        lap = lap + shifted(g, 1, before, after) + shifted(g, 2) - 6.0 * g
        out = keep(g + (dif[v] * lap + made[v]), has_x)
        gx_ref[pl.ds(v * 2 * rows_y, 2 * rows_y), :] = out.reshape(2 * rows_y, lanes)
        at = pl.ds(v * size, rows_y)
        sec[at, :] = sec[at, :] + dif[v] * g[0]
        at = pl.ds(v * size + size - rows_y, rows_y)
        sec[at, :] = sec[at, :] + dif[v] * g[1]

    def emit(v, x, n, w, t):
        at = pl.ds(v * size + x * rows_y, n * rows_y)
        state_ref[at, :] = 0.5 * ((f_ref[at, :] + w.reshape(n * rows_y, lanes)) + t.reshape(n * rows_y, lanes))

    stage(
        sec, lambda v, x: v * size + x * rows_y, nv, rows_x, rows_y, (dif, pre, act, mix), emit,
        lambda v: gx_ref[pl.ds(v * 2 * rows_y, rows_y), :][None],
        lambda v: gx_ref[pl.ds((v * 2 + 1) * rows_y, rows_y), :][None],
    )
    total = None
    for v in range(nv):
        half = 0.5 * dif[v]
        at = pl.ds(v * size, rows_x, stride=rows_y)
        state_ref[at, :] = state_ref[at, :] + half * gy_ref[pl.ds(v * 2 * rows_x, rows_x), :]
        at = pl.ds(v * size + rows_y - 1, rows_x, stride=rows_y)
        state_ref[at, :] = state_ref[at, :] + half * gy_ref[pl.ds((v * 2 + 1) * rows_x, rows_x), :]
        at = pl.ds(v * lanes, lanes)
        part = mm3(split(state_ref[pl.ds(v * size, size), :]), (kh[at, :], kl[at, :]))
        total = part if total is None else total + part
    pack_message(m_ref, total, bx_ref[...])


def dense(size, width, rows_x, rank_x, lanes):
    return width % lanes * 2 == lanes and rank_x * 2 == lanes and size % 16 == 0 and rows_x % 16 == 0


def message_shape(size, width, rows_x, rank_x, lanes):
    if not dense(size, width, rows_x, rank_x, lanes):
        return (size + rows_x, max(width, rank_x))
    return (size * (width // lanes) + size // 2 + rows_x // 2, lanes)


def fold(a):
    half = a.shape[0] // 2
    return jnp.concatenate([a[:half], a[half:]], axis=1)


def unfold(a):
    half = a.shape[1] // 2
    return jnp.concatenate([a[:, :half], a[:, half:]], axis=0)


def pack_message(m_ref, values, basis):
    size, width = values.shape
    lanes = m_ref.shape[1]
    if not dense(size, width, *basis.shape, lanes):
        m_ref[:size, :width] = values
        m_ref[size:, : basis.shape[1]] = basis
        return
    whole = width // lanes
    for i in range(whole):
        m_ref[pl.ds(i * size, size), :] = values[:, i * lanes : (i + 1) * lanes]
    m_ref[pl.ds(whole * size, size // 2), :] = fold(values[:, whole * lanes :])
    m_ref[pl.ds(whole * size + size // 2, basis.shape[0] // 2), :] = fold(basis)


def unpack_message(m_ref, size, width, rows_x, rank_x):
    lanes = m_ref.shape[1]
    if not dense(size, width, rows_x, rank_x, lanes):
        return m_ref[:size, :width], m_ref[size:, :rank_x]
    whole = width // lanes
    parts = [m_ref[pl.ds(i * size, size), :] for i in range(whole)]
    parts.append(unfold(m_ref[pl.ds(whole * size, size // 2), :]))
    basis = unfold(m_ref[pl.ds(whole * size + size // 2, rows_x // 2), :])
    return jnp.concatenate(parts, axis=1), basis


def mix_blocks(sizes, refs):
    rows_x, rows_y, width, rank_x = sizes
    size = rows_x * rows_y
    same = place((size, size), 0) % rows_y == place((size, size), 1) % rows_y

    def repeated(basis):
        return jnp.broadcast_to(basis[:, None, :], (rows_x, rows_y, rank_x)).reshape(size, rank_x)

    own = total = None
    for ref in refs:
        values, basis = unpack_message(ref, size, width, rows_x, rank_x)
        basis = repeated(basis)
        own = basis if own is None else own
        link = lax.dot_general(
            own, basis, (((1,), (1,)), ((), ())), precision=HIGH, preferred_element_type=jnp.float32
        )
        part = mm3(split(jnp.where(same, link, 0.0)), split(values))
        total = part if total is None else total + part
    return total


def lane_sums(row, group, shift, lanes):
    shape = (row.shape[1], lanes)
    pick = (place(shape, 0) // group + shift == place(shape, 1)).astype(jnp.float32)
    return jnp.dot(row, pick, precision=HIGH, preferred_element_type=jnp.float32)


def side_kernel(dims, state_ref, bz_ref, w_ref, row_ref):
    nv, rows_x, rows_y, lanes = dims
    size = rows_x * rows_y
    bz = split(bz_ref[...])
    row = jnp.zeros(row_ref.shape, jnp.float32)
    ones = jnp.ones((8, lanes), jnp.float32)
    made = []
    for v in range(nv):
        state = state_ref[pl.ds(v * size, size), :]
        part = mm3(split(state), bz, True)
        made.append(part)
        rest = state - mm3(split(part), bz)
        outside = jnp.sum(rest * rest, axis=0, keepdims=True)
        square = jnp.sum(state * state, axis=0, keepdims=True)
        row = row + lane_sums(outside, lanes, v, lanes) + lane_sums(square, lanes, nv + v, lanes)
    w_ref[...] = jnp.concatenate(made, axis=1)
    row_ref[...] = row


def settle(mixed, w_ref, row_ref, uh, ul, sums_ref, rank_z):
    gap = w_ref[...] - mm3(split(mixed), (uh[...], ul[...]))
    row = row_ref[...] + lane_sums(jnp.sum(gap * gap, axis=0, keepdims=True), rank_z, 0, row_ref.shape[1])
    sums_ref[...] = jnp.broadcast_to(row, sums_ref.shape)


def third_kernel(sizes, rank_z, n, *refs):
    w_ref, row_ref, uh, ul, d_ref, sums_ref = refs[n:]
    mixed = mix_blocks(sizes, refs[:n])
    d_ref[...] = mixed
    settle(mixed, w_ref, row_ref, uh, ul, sums_ref, rank_z)


def mix_kernel(sizes, n, *refs):
    refs[n][...] = mix_blocks(sizes, refs[:n])


def settle_kernel(rank_z, d_ref, w_ref, row_ref, uh, ul, sums_ref):
    settle(d_ref[...], w_ref, row_ref, uh, ul, sums_ref, rank_z)


def decode_kernel(dims, d_ref, th, tl, recon_ref):
    nv, rows_x, rows_y, lanes = dims
    size = rows_x * rows_y
    halves = split(d_ref[...])
    for v in range(nv):
        cols = slice(v * lanes, (v + 1) * lanes)
        recon_ref[pl.ds(v * size, size), :] = mm3(halves, (th[:, cols], tl[:, cols]))


def pairs(n, first):
    swaps = [(i, i + 1) for i in range(first, n - 1, 2)]
    return swaps + [(j, i) for i, j in swaps]


def gather_blocks(block):
    n = lax.axis_size("gx")
    if n & (n - 1):
        every = lax.all_gather(block, "gx", axis=0)
        return [block] + [jnp.roll(every, -lax.axis_index("gx"), 0)[i] for i in range(1, n)]
    blocks = [block]
    bit = n // 2
    while bit:
        swaps = [(i, i ^ bit) for i in range(n)]
        blocks = blocks + [lax.ppermute(b, "gx", swaps) for b in blocks]
        bit //= 2
    return blocks


def program(field, diffusion, prefactor, activation, mixing, basis_x, basis_y, basis_z, basis_v):
    f32, bf16 = jnp.float32, jnp.bfloat16
    dims = field.shape
    nv, rows_x, rows_y, lanes = dims
    size = rows_x * rows_y
    rank_x, rank_z, rank_v = basis_x.shape[1], basis_z.shape[1], basis_v.shape[1]
    width, part = rank_z * rank_v, nv * rank_z
    gx, gy = lax.axis_size("gx"), lax.axis_size("gy")
    peers = gx * gy
    coeffs = (diffusion, prefactor, activation, mixing)
    flat = field.reshape(nv * size, lanes)
    block = (nv * size, lanes)

    y_msg, x_msg = (2 * nv * rows_x, lanes), (2 * nv * rows_y, lanes)
    p1, p2, q1, q2 = call(
        functools.partial(pack_kernel, dims), [(y_msg, f32)] * 2 + [(x_msg, f32)] * 2, [VM]
    )(flat)
    x1 = lax.ppermute(q1, "gx", pairs(gx, 0))
    x2 = lax.ppermute(q2, "gx", pairs(gx, 1))
    y1 = lax.ppermute(p1, "gy", pairs(gy, 0))
    y2 = lax.ppermute(p2, "gy", pairs(gy, 1))
    c1, c2 = call(
        functools.partial(corner_kernel, dims), [((2 * nv, lanes), f32)] * 2, [VM] * 2
    )(x1, x2)
    c1 = lax.ppermute(c1, "gy", pairs(gy, 0))
    c2 = lax.ppermute(c2, "gy", pairs(gy, 1))

    section, kh, kl, th, tl, uh, ul = call(
        functools.partial(first_kernel, dims),
        [(block, f32)]
        + [((nv * lanes, width), bf16)] * 2
        + [((width, nv * lanes), bf16)] * 2
        + [((width, part), bf16)] * 2,
        [VM] * 3 + [SM] * 4,
    )(flat, basis_z.T, basis_v.T, *coeffs)
    state, message = call(
        functools.partial(second_kernel, dims),
        [(block, f32), (message_shape(size, width, rows_x, rank_x, lanes), f32)],
        [VM] * 11 + [SM] * 4,
        [
            pltpu.VMEM(block, f32),
            pltpu.VMEM((nv * 2 * rows_x, lanes), f32),
            pltpu.VMEM((nv * 2 * rows_y, lanes), f32),
        ],
    )(flat, section, y1, y2, x1, x2, c1, c2, basis_x, kh, kl, *coeffs)
    blocks = gather_blocks(message)
    n = len(blocks)
    coefs, row = call(
        functools.partial(side_kernel, dims), [((size, part), f32), ((1, lanes), f32)], [VM] * 2
    )(state, basis_z.T)
    sizes = (rows_x, rows_y, width, rank_x)
    outs = [((size, width), f32), ((peers, lanes), f32)]
    if basis_y.shape[0] * gy == basis_y.shape[1]:
        mixed, sums = call(
            functools.partial(third_kernel, sizes, rank_z, n), outs, [VM] * (n + 4)
        )(*blocks, coefs, row, uh, ul)
    else:
        (mixed,) = call(functools.partial(mix_kernel, sizes, n), outs[:1], [VM] * n)(*blocks)
        mixed = mixed.reshape(rows_x, rows_y, width)
        core = lax.psum(jnp.einsum("xyk,yb->xbk", mixed, basis_y, precision=HIGH), "gy")
        mixed = jnp.einsum("xbk,yb->xyk", core, basis_y, precision=HIGH).reshape(size, width)
        (sums,) = call(functools.partial(settle_kernel, rank_z), outs[1:], [VM] * 5)(
            mixed, coefs, row, uh, ul
        )
    (recon,) = call(functools.partial(decode_kernel, dims), [(block, f32)], [VM] * 3)(mixed, th, tl)
    if peers > 64:
        sums = lax.psum(sums[0], ("gx", "gy"))
    else:
        sums = jnp.sum(lax.all_to_all(sums, ("gx", "gy"), 0, 0, tiled=True), axis=0)
    residual = jnp.sqrt(sums[:nv] / (sums[nv : 2 * nv] + 1e-06))
    return (state.reshape(dims), recon.reshape(dims), residual)


def solution(mesh):
    return jax.shard_map(
        program,
        mesh=mesh,
        in_specs=(
            P(None, "gx", "gy", None),
            P(),
            P(),
            P(),
            P(),
            P("gx", None),
            P("gy", None),
            P(),
            P(),
        ),
        out_specs=(P(None, "gx", "gy", None), P(None, "gx", "gy", None), P()),
        check_vma=False,
    )
```

```python
import functools

import jax
import jax.numpy as jnp
from jax import lax
from jax.experimental import pallas as pl
from jax.experimental.pallas import tpu as pltpu
from jax.sharding import PartitionSpec as P


HIGH = lax.Precision.HIGHEST
VM = pl.BlockSpec(memory_space=pltpu.VMEM)
SM = pl.BlockSpec(memory_space=pltpu.SMEM)


def call(kernel, outs, in_specs, scratch=(), flops=10**7, vmem=12, out_specs=None):
    return pl.pallas_call(
        kernel,
        out_shape=[jax.ShapeDtypeStruct(s, d) for s, d in outs],
        in_specs=in_specs,
        out_specs=out_specs or [VM] * len(outs),
        scratch_shapes=list(scratch),
        compiler_params=pltpu.CompilerParams(vmem_limit_bytes=vmem << 20),
        cost_estimate=pl.CostEstimate(flops=flops, bytes_accessed=10**6, transcendentals=0),
    )


def split(a):
    hi = a.astype(jnp.bfloat16)
    lo = (a - hi.astype(jnp.float32)).astype(jnp.bfloat16)
    return hi, lo


def mm(a, b, nt=False):
    dims = (((1,), (1 if nt else 0,)), ((), ()))
    return lax.dot_general(a, b, dims, preferred_element_type=jnp.float32)


def mm3(a, b, nt=False):
    return mm(a[0], b[0], nt) + mm(a[0], b[1], nt) + mm(a[1], b[0], nt)


def place(shape, dim):
    return lax.broadcasted_iota(jnp.int32, shape, dim)


def shifted(w, axis, before=0.0, after=0.0):
    size = w.shape[axis]
    pos = place(w.shape, axis)
    low = jnp.where(pos == 0, before, pltpu.roll(w, 1, axis))
    high = jnp.where(pos == size - 1, after, pltpu.roll(w, size - 1, axis))
    return low + high


def tiles_of(a):
    return a.reshape(a.size // (8 * a.shape[-1]), 8, a.shape[-1])


def reaction(ws, act, both, low):
    n = len(ws)
    cold = -1.0 / (1.5 + jnp.tanh(ws[0]))
    rates = [tiles_of(jnp.exp(act[v] * cold) * ws[v]) for v in range(n)]
    count, lanes = rates[0].shape[0], rates[0].shape[2]
    stacked = jnp.concatenate(
        [jnp.concatenate([rates[v][t] for v in range(n)], axis=0) for t in range(count)], axis=1
    )
    hi, lo = split(stacked)
    out = mm(both, jnp.concatenate([hi, lo], axis=0)) + mm(low, hi)
    return [
        jnp.stack([out[v * 8 : (v + 1) * 8, t * lanes : (t + 1) * lanes] for t in range(count)]).reshape(ws[v].shape)
        for v in range(n)
    ]


def stage(ref, nv, rows_x, rows_y, dif, act, mixers, emit, low_edge, high_edge, step=4):
    lanes = ref.shape[1]
    size = rows_x * rows_y

    def rows(v, x, n):
        return ref[pl.ds(v * size + x * rows_y, n * rows_y), :].reshape(n, rows_y, lanes)

    step = min(step, rows_x)
    for x in range(0, rows_x, step):
        ws = [rows(v, x, step) for v in range(nv)]
        made = reaction(ws, act, *mixers)
        for v in range(nv):
            w = ws[v]
            first = rows(v, x - 1, 1) if x > 0 else low_edge(v)[None]
            last = rows(v, x + step, 1) if x + step < rows_x else high_edge(v)[None]
            beside = jnp.concatenate([first, w[:-1]], 0) + jnp.concatenate([w[1:], last], 0)
            lap = beside + shifted(w, 1) + shifted(w, 2) - 6.0 * w
            emit(v, x, step, w, dif[v] * lap + made[v])


def odd(axis):
    return lax.axis_index(axis) % 2 == 1


def two(one, other, is_odd, at):
    a, b = one[at, :], other[at, :]
    return jnp.where(is_odd, a, b), jnp.where(is_odd, b, a)


def pack_x_kernel(dims, f_ref, q1, q2):
    nv, rows_x, rows_y, _ = dims
    size = rows_x * rows_y
    for layer in range(2):
        for v in range(nv):
            low = f_ref[pl.ds(v * size + layer * rows_y, rows_y), :]
            high = f_ref[pl.ds(v * size + (rows_x - 1 - layer) * rows_y, rows_y), :]
            at = pl.ds((layer * nv + v) * rows_y, rows_y)
            q1[at, :] = jnp.where(odd("gx"), low, high)
            q2[at, :] = jnp.where(odd("gx"), high, low)


def pack_y_kernel(dims, f_ref, x1, x2, p1, p2):
    nv, rows_x, rows_y, _ = dims
    size = rows_x * rows_y

    def put(at, low, high):
        p1[at, :] = jnp.where(odd("gy"), low, high)
        p2[at, :] = jnp.where(odd("gy"), high, low)

    for layer in range(2):
        for v in range(nv):
            low = f_ref[pl.ds(v * size + layer, rows_x, stride=rows_y), :]
            high = f_ref[pl.ds(v * size + rows_y - 1 - layer, rows_x, stride=rows_y), :]
            put(pl.ds((layer * nv + v) * rows_x, rows_x), low, high)
    lows = two(x1, x2, odd("gx"), pl.ds(0, nv, stride=rows_y))
    highs = two(x1, x2, odd("gx"), pl.ds(rows_y - 1, nv, stride=rows_y))
    for side in range(2):
        put(pl.ds((2 * rows_x + side) * nv, nv), lows[side], highs[side])


def first_kernel(dims, f_ref, x1, x2, bz_ref, bv_ref, mix_ref, dif, pre, act, *outs):
    s_ref, k_ref, t_ref, u_ref, n_ref, both_ref, low_ref = outs
    nv, rows_x, rows_y, lanes = dims
    size = rows_x * rows_y
    spot = place((nv, nv), 1)
    scaled = mix_ref[...]
    for u in range(nv):
        scaled = jnp.where(spot == u, scaled * pre[u], scaled)
    wide = (nv * 8, nv)
    spread = (place(wide, 0) // 8 == place(wide, 1)).astype(jnp.float32)
    full = jnp.dot(spread, scaled, precision=HIGH, preferred_element_type=jnp.float32)
    full = lax.dot_general(
        full, spread, (((1,), (1,)), ((), ())), precision=HIGH, preferred_element_type=jnp.float32
    )
    hi, lo = split(jnp.where(place(full.shape, 0) % 8 == place(full.shape, 1) % 8, full, 0.0))
    both = jnp.concatenate([hi, hi], axis=1)
    both_ref[...], low_ref[...] = both, lo

    def emit(v, x, n, w, t):
        s_ref[pl.ds(v * size + x * rows_y, n * rows_y), :] = (w + t).reshape(n * rows_y, lanes)

    def edge(side):
        return lambda v: two(x1, x2, odd("gx"), pl.ds(v * rows_y, rows_y))[side]

    stage(f_ref, nv, rows_x, rows_y, dif, act, (both, lo), emit, edge(0), edge(1))
    bz, bv = bz_ref[...], bv_ref[...]
    rank_z, rank_v = bz.shape[0], bv.shape[0]
    width, part = rank_z * rank_v, nv * rank_z
    pick_z = (place((rank_z, width), 1) % rank_z == place((rank_z, width), 0)).astype(jnp.float32)
    pick_v = (place((rank_v, width), 1) // rank_z == place((rank_v, width), 0)).astype(jnp.float32)
    first = (((0,), (0,)), ((), ()))
    wide_z = lax.dot_general(bz, pick_z, first, precision=HIGH, preferred_element_type=jnp.float32)
    wide_v = lax.dot_general(bv, pick_v, first, precision=HIGH, preferred_element_type=jnp.float32)
    for v in range(nv):
        product = wide_z * wide_v[v : v + 1, :]
        at = slice(v * lanes, (v + 1) * lanes)
        k_ref[0, at, :], k_ref[1, at, :] = split(product)
        t_ref[0, :, at], t_ref[1, :, at] = split(product.T)
    pick_u = (place((nv, part), 1) // rank_z == place((nv, part), 0)).astype(jnp.float32)
    tall = lax.dot_general(pick_v, bv, first, precision=HIGH, preferred_element_type=jnp.float32)
    tall = jnp.dot(tall, pick_u, precision=HIGH, preferred_element_type=jnp.float32)
    same = place((width, part), 0) % rank_z == place((width, part), 1) % rank_z
    u_ref[0], u_ref[1] = split(jnp.where(same, tall, 0.0))
    held = lanes // rank_z
    spread = (place((rank_z, lanes), 1) % rank_z == place((rank_z, lanes), 0)).astype(jnp.float32)
    wide_z = lax.dot_general(bz, spread, first, precision=HIGH, preferred_element_type=jnp.float32)
    group = place((lanes, lanes), 1) // rank_z
    for j in range(held):
        at = slice(j * lanes, (j + 1) * lanes)
        n_ref[0, at, :], n_ref[1, at, :] = split(jnp.where(group == j, wide_z, 0.0))


def second_kernel(
    dims, f_ref, s_ref, y1, y2, x1, x2, bx_ref, k_ref, both_ref, low_ref, dif, act,
    state_ref, m_ref, sec, gy_ref, gx_ref,
):
    nv, rows_x, rows_y, lanes = dims
    size = rows_x * rows_y
    ix, iy = lax.axis_index("gx"), lax.axis_index("gy")
    has_x = (ix > 0, ix < lax.axis_size("gx") - 1)
    has_y = (iy > 0, iy < lax.axis_size("gy") - 1)
    mixers = (both_ref[...], low_ref[...])

    def y_ghost(layer, v):
        return jnp.stack(two(y1, y2, odd("gy"), pl.ds((layer * nv + v) * rows_x, rows_x)))

    def x_ghost(layer, v):
        return jnp.stack(two(x1, x2, odd("gx"), pl.ds((layer * nv + v) * rows_y, rows_y)))

    def corner(side, v):
        return two(y1, y2, odd("gy"), pl.ds((2 * rows_x + side) * nv + v, 1))

    def keep(value, flags):
        inside = [jnp.where(flags[i], value[i], 0.0) for i in range(2)]
        return jnp.concatenate(inside, axis=0)

    ys = [y_ghost(0, v) for v in range(nv)]
    xs = [x_ghost(0, v) for v in range(nv)]
    made = reaction([jnp.concatenate([tiles_of(ys[v]), tiles_of(xs[v])], 0) for v in range(nv)], act, *mixers)
    for v in range(nv):
        g = ys[v]
        cut = g.size // (8 * lanes)
        low = f_ref[pl.ds(v * size, rows_x, stride=rows_y), :]
        high = f_ref[pl.ds(v * size + rows_y - 1, rows_x, stride=rows_y), :]
        left, right = corner(0, v), corner(1, v)
        lap = y_ghost(1, v) + jnp.stack([low, high]) - 6.0 * g
        lap = lap + shifted(g, 1, jnp.stack(left), jnp.stack(right)) + shifted(g, 2)
        out = g + (dif[v] * lap + made[v][:cut].reshape(g.shape))
        gy_ref[pl.ds(v * 2 * rows_x, 2 * rows_x), :] = keep(out, has_y)
        sec[pl.ds(v * size, size), :] = s_ref[pl.ds(v * size, size), :]
        at = pl.ds(v * size, rows_x, stride=rows_y)
        sec[at, :] = sec[at, :] + dif[v] * g[0]
        at = pl.ds(v * size + rows_y - 1, rows_x, stride=rows_y)
        sec[at, :] = sec[at, :] + dif[v] * g[1]
        g = xs[v]
        low = f_ref[pl.ds(v * size, rows_y), :]
        high = f_ref[pl.ds(v * size + size - rows_y, rows_y), :]
        before = jnp.stack([left[0], right[0]])
        after = jnp.stack([left[1], right[1]])
        lap = x_ghost(1, v) + jnp.stack([low, high]) - 6.0 * g
        lap = lap + shifted(g, 1, before, after) + shifted(g, 2)
        out = g + (dif[v] * lap + made[v][cut:].reshape(g.shape))
        gx_ref[pl.ds(v * 2 * rows_y, 2 * rows_y), :] = keep(out, has_x)

    def emit(v, x, n, w, t):
        at = pl.ds(v * size + x * rows_y, n * rows_y)
        state_ref[at, :] = 0.5 * ((f_ref[at, :] + w.reshape(n * rows_y, lanes)) + t.reshape(n * rows_y, lanes))

    stage(
        sec, nv, rows_x, rows_y, dif, act, mixers, emit,
        lambda v: gx_ref[pl.ds(v * 2 * rows_y, rows_y), :],
        lambda v: gx_ref[pl.ds((v * 2 + 1) * rows_y, rows_y), :],
    )
    his, los = [], []
    for v in range(nv):
        half = 0.5 * dif[v]
        at = pl.ds(v * size, rows_x, stride=rows_y)
        state_ref[at, :] = state_ref[at, :] + half * gy_ref[pl.ds(v * 2 * rows_x, rows_x), :]
        at = pl.ds(v * size + rows_y - 1, rows_x, stride=rows_y)
        state_ref[at, :] = state_ref[at, :] + half * gy_ref[pl.ds((v * 2 + 1) * rows_x, rows_x), :]
        hi, lo = split(state_ref[pl.ds(v * size, size), :])
        his.append(hi)
        los.append(lo)
    total = mm3((jnp.concatenate(his, 1), jnp.concatenate(los, 1)), (k_ref[0], k_ref[1]))
    pack_message(m_ref, total, bx_ref[...])


def dense(size, width, rows_x, rank_x, lanes):
    return width % lanes * 2 == lanes and rank_x * 2 == lanes and size % 16 == 0 and rows_x % 16 == 0


def message_shape(size, width, rows_x, rank_x, lanes):
    if not dense(size, width, rows_x, rank_x, lanes):
        return (size + rows_x, max(width, rank_x))
    return (size * (width // lanes) + size // 2 + rows_x // 2, lanes)


def fold(a):
    half = a.shape[0] // 2
    return jnp.concatenate([a[:half], a[half:]], axis=1)


def unfold(a):
    half = a.shape[1] // 2
    return jnp.concatenate([a[:, :half], a[:, half:]], axis=0)


def pack_message(m_ref, values, basis):
    size, width = values.shape
    lanes = m_ref.shape[1]
    if not dense(size, width, *basis.shape, lanes):
        m_ref[:size, :width] = values
        m_ref[size:, : basis.shape[1]] = basis
        return
    whole = width // lanes
    for i in range(whole):
        m_ref[pl.ds(i * size, size), :] = values[:, i * lanes : (i + 1) * lanes]
    m_ref[pl.ds(whole * size, size // 2), :] = fold(values[:, whole * lanes :])
    m_ref[pl.ds(whole * size + size // 2, basis.shape[0] // 2), :] = fold(basis)


def unpack_message(m_ref, size, width, rows_x, rank_x):
    lanes = m_ref.shape[1]
    if not dense(size, width, rows_x, rank_x, lanes):
        return m_ref[:size, :width], m_ref[size:, :rank_x]
    whole = width // lanes
    parts = [m_ref[pl.ds(i * size, size), :] for i in range(whole)]
    parts.append(unfold(m_ref[pl.ds(whole * size, size // 2), :]))
    basis = unfold(m_ref[pl.ds(whole * size + size // 2, rows_x // 2), :])
    return jnp.concatenate(parts, axis=1), basis


def mix_blocks(sizes, refs):
    rows_x, rows_y, width, rank_x = sizes
    size = rows_x * rows_y

    def repeated(basis):
        return jnp.broadcast_to(basis[:, None, :], (rows_x, rows_y, rank_x)).reshape(size, rank_x)

    parts = [unpack_message(ref, size, width, rows_x, rank_x) for ref in refs]
    values = jnp.concatenate([values for values, _ in parts], axis=0)
    bases = jnp.concatenate([repeated(basis) for _, basis in parts], axis=0)
    hi, lo = split(bases)
    link = mm3((hi[:size], lo[:size]), (hi, lo), True)
    same = place(link.shape, 0) % rows_y == place(link.shape, 1) % rows_y
    return mm3(split(jnp.where(same, link, 0.0)), split(values))


def side_kernel(dims, rank_z, state_ref, n_ref, out_ref, w_ref, row_ref, sem):
    nv, rows_x, rows_y, lanes = dims
    size = rows_x * rows_y
    write = pltpu.make_async_copy(state_ref, out_ref, sem)
    write.start()
    held = lanes // rank_z
    basis = (n_ref[0], n_ref[1])

    def squares(a):
        return jnp.sum((a * a).reshape(size // 8, 8, lanes), axis=0)

    outside, mass = [], []
    for v in range(0, nv, held):
        state = jnp.concatenate([state_ref[pl.ds((v + j) * size, size), :] for j in range(held)], axis=1)
        coefs = mm3(split(state), basis)
        w_ref[:, (v // held) * lanes : (v // held + 1) * lanes] = coefs
        rest = state - mm3(split(coefs), basis, True)
        for j in range(held):
            outside.append(squares(rest[:, j * lanes : (j + 1) * lanes]))
            mass.append(squares(state[:, j * lanes : (j + 1) * lanes]))
    every = jnp.concatenate(outside + mass, axis=0)
    ones = jnp.ones((8, lanes), jnp.float32)
    sums = lax.dot_general(
        ones, every, (((1,), (1,)), ((), ())), precision=HIGH, preferred_element_type=jnp.float32
    )
    shape = (every.shape[0], row_ref.shape[1])
    pick = (place(shape, 0) // 8 == place(shape, 1)).astype(jnp.float32)
    row_ref[...] = jnp.dot(sums, pick, precision=HIGH, preferred_element_type=jnp.float32)
    write.wait()


def settle(mixed, w_ref, row_ref, u_ref, sums_ref, rank_z):
    gap = w_ref[...] - mm3(split(mixed), (u_ref[0], u_ref[1]))
    size, part = gap.shape
    hi, lo = split(jnp.sum((gap * gap).reshape(size // 8, 8, part), axis=0))
    shape = (part, row_ref.shape[1])
    pick = (place(shape, 0) // rank_z == place(shape, 1)).astype(jnp.float32).astype(jnp.bfloat16)
    row = jnp.sum(mm(hi, pick) + mm(lo, pick), axis=0, keepdims=True) + row_ref[0:1, :]
    sums_ref[...] = jnp.broadcast_to(row, sums_ref.shape)


def third_kernel(sizes, rank_z, n, *refs):
    w_ref, row_ref, u_ref, d_ref, sums_ref = refs[n:]
    mixed = mix_blocks(sizes, refs[:n])
    d_ref[...] = mixed
    settle(mixed, w_ref, row_ref, u_ref, sums_ref, rank_z)


def mix_kernel(sizes, n, *refs):
    refs[n][...] = mix_blocks(sizes, refs[:n])


def settle_kernel(rank_z, d_ref, w_ref, row_ref, u_ref, sums_ref):
    settle(d_ref[...], w_ref, row_ref, u_ref, sums_ref, rank_z)


def decode_kernel(dims, d_ref, t_ref, recon_ref):
    nv, rows_x, rows_y, lanes = dims
    size = rows_x * rows_y
    halves = split(d_ref[...])
    for v in range(nv):
        cols = slice(v * lanes, (v + 1) * lanes)
        recon_ref[pl.ds(v * size, size), :] = mm3(halves, (t_ref[0, :, cols], t_ref[1, :, cols]))


def pairs(n, first):
    swaps = [(i, i + 1) for i in range(first, n - 1, 2)]
    return swaps + [(j, i) for i, j in swaps]


def gather_blocks(block):
    n = lax.axis_size("gx")
    if n & (n - 1):
        every = lax.all_gather(block, "gx", axis=0)
        return [block] + [jnp.roll(every, -lax.axis_index("gx"), 0)[i] for i in range(1, n)]
    blocks = [block]
    bit = n // 2
    while bit:
        swaps = [(i, i ^ bit) for i in range(n)]
        blocks = blocks + [lax.ppermute(b, "gx", swaps) for b in blocks]
        bit //= 2
    return blocks


def program(field, diffusion, prefactor, activation, mixing, basis_x, basis_y, basis_z, basis_v):
    f32, bf16 = jnp.float32, jnp.bfloat16
    dims = field.shape
    nv, rows_x, rows_y, lanes = dims
    size = rows_x * rows_y
    rank_x, rank_z, rank_v = basis_x.shape[1], basis_z.shape[1], basis_v.shape[1]
    width, part = rank_z * rank_v, nv * rank_z
    gx, gy = lax.axis_size("gx"), lax.axis_size("gy")
    peers = gx * gy
    flat = field.reshape(nv * size, lanes)
    block = (nv * size, lanes)

    y_msg, x_msg = (2 * nv * (rows_x + 1), lanes), (2 * nv * rows_y, lanes)
    q1, q2 = call(functools.partial(pack_x_kernel, dims), [(x_msg, f32)] * 2, [VM])(flat)
    x1 = lax.ppermute(q1, "gx", pairs(gx, 0))
    x2 = lax.ppermute(q2, "gx", pairs(gx, 1))
    p1, p2 = call(functools.partial(pack_y_kernel, dims), [(y_msg, f32)] * 2, [VM] * 3)(flat, x1, x2)
    y1 = lax.ppermute(p1, "gy", pairs(gy, 0))
    y2 = lax.ppermute(p2, "gy", pairs(gy, 1))

    section, k, t, u, n, both, low = call(
        functools.partial(first_kernel, dims),
        [
            (block, f32),
            ((2, nv * lanes, width), bf16),
            ((2, width, nv * lanes), bf16),
            ((2, width, part), bf16),
            ((2, lanes // rank_z * lanes, lanes), bf16),
            ((nv * 8, nv * 16), bf16),
            ((nv * 8, nv * 8), bf16),
        ],
        [VM] * 6 + [SM] * 3,
    )(flat, x1, x2, basis_z.T, basis_v.T, mixing, diffusion, prefactor, activation)
    state, message = call(
        functools.partial(second_kernel, dims),
        [(block, f32), (message_shape(size, width, rows_x, rank_x, lanes), f32)],
        [VM] * 10 + [SM] * 2,
        [
            pltpu.VMEM(block, f32),
            pltpu.VMEM((nv * 2 * rows_x, lanes), f32),
            pltpu.VMEM((nv * 2 * rows_y, lanes), f32),
        ],
    )(flat, section, y1, y2, x1, x2, basis_x, k, both, low, diffusion, activation)
    blocks = gather_blocks(message)
    count = len(blocks)
    state, coefs, row = call(
        functools.partial(side_kernel, dims, rank_z),
        [(block, f32), ((size, part), f32), ((8, lanes), f32)],
        [VM] * 2,
        [pltpu.SemaphoreType.DMA],
        out_specs=[pl.BlockSpec(memory_space=pl.ANY), VM, VM],
    )(state, n)
    sizes = (rows_x, rows_y, width, rank_x)
    outs = [((size, width), f32), ((peers, lanes), f32)]
    if basis_y.shape[0] * gy == basis_y.shape[1]:
        mixed, sums = call(
            functools.partial(third_kernel, sizes, rank_z, count), outs, [VM] * (count + 3)
        )(*blocks, coefs, row, u)
    else:
        (mixed,) = call(functools.partial(mix_kernel, sizes, count), outs[:1], [VM] * count)(*blocks)
        mixed = mixed.reshape(rows_x, rows_y, width)
        core = lax.psum(jnp.einsum("xyk,yb->xbk", mixed, basis_y, precision=HIGH), "gy")
        mixed = jnp.einsum("xbk,yb->xyk", core, basis_y, precision=HIGH).reshape(size, width)
        (sums,) = call(functools.partial(settle_kernel, rank_z), outs[1:], [VM] * 4)(mixed, coefs, row, u)
    (recon,) = call(functools.partial(decode_kernel, dims), [(block, f32)], [VM] * 2)(mixed, t)
    if peers > 64:
        sums = lax.psum(sums[0], ("gx", "gy"))
    else:
        sums = jnp.sum(lax.all_to_all(sums, ("gx", "gy"), 0, 0, tiled=True), axis=0)
    residual = jnp.sqrt(sums[:nv] / (sums[nv : 2 * nv] + 1e-06))
    return (state.reshape(dims), recon.reshape(dims), residual)


def solution(mesh):
    return jax.shard_map(
        program,
        mesh=mesh,
        in_specs=(
            P(None, "gx", "gy", None),
            P(),
            P(),
            P(),
            P(),
            P("gx", None),
            P("gy", None),
            P(),
            P(),
        ),
        out_specs=(P(None, "gx", "gy", None), P(None, "gx", "gy", None), P()),
        check_vma=False,
    )
```

```python
import functools

import jax
import jax.numpy as jnp
from jax import lax
from jax.experimental import pallas as pl
from jax.experimental.pallas import tpu as pltpu
from jax.sharding import PartitionSpec as P


HIGH = lax.Precision.HIGHEST
VM = pl.BlockSpec(memory_space=pltpu.VMEM)
SM = pl.BlockSpec(memory_space=pltpu.SMEM)


def call(kernel, outs, in_specs, scratch=(), flops=10**7, vmem=12, out_specs=None):
    return pl.pallas_call(
        kernel,
        out_shape=[jax.ShapeDtypeStruct(s, d) for s, d in outs],
        in_specs=in_specs,
        out_specs=out_specs or [VM] * len(outs),
        scratch_shapes=list(scratch),
        compiler_params=pltpu.CompilerParams(vmem_limit_bytes=vmem << 20),
        cost_estimate=pl.CostEstimate(flops=flops, bytes_accessed=10**6, transcendentals=0),
    )


def split(a):
    hi = a.astype(jnp.bfloat16)
    lo = (a - hi.astype(jnp.float32)).astype(jnp.bfloat16)
    return hi, lo


def mm(a, b, nt=False):
    dims = (((1,), (1 if nt else 0,)), ((), ()))
    return lax.dot_general(a, b, dims, preferred_element_type=jnp.float32)


def mm3(a, b, nt=False):
    return mm(a[0], b[0], nt) + mm(a[0], b[1], nt) + mm(a[1], b[0], nt)


def place(shape, dim):
    return lax.broadcasted_iota(jnp.int32, shape, dim)


def shifted(w, axis, before=0.0, after=0.0):
    size = w.shape[axis]
    pos = place(w.shape, axis)
    low = jnp.where(pos == 0, before, pltpu.roll(w, 1, axis))
    high = jnp.where(pos == size - 1, after, pltpu.roll(w, size - 1, axis))
    return low + high


def tiles_of(a):
    return a.reshape(a.size // (8 * a.shape[-1]), 8, a.shape[-1])


def reaction(ws, act, both, low):
    n = len(ws)
    cold = -1.0 / (1.5 + jnp.tanh(ws[0]))
    rates = [tiles_of(jnp.exp(act[v] * cold) * ws[v]) for v in range(n)]
    count, lanes = rates[0].shape[0], rates[0].shape[2]
    stacked = jnp.concatenate(
        [jnp.concatenate([rates[v][t] for v in range(n)], axis=0) for t in range(count)], axis=1
    )
    hi, lo = split(stacked)
    out = mm(both, jnp.concatenate([hi, lo], axis=0)) + mm(low, hi)
    return [
        jnp.stack([out[v * 8 : (v + 1) * 8, t * lanes : (t + 1) * lanes] for t in range(count)]).reshape(ws[v].shape)
        for v in range(n)
    ]


def stage(ref, nv, rows_x, rows_y, dif, act, mixers, emit, low_edge, high_edge, step=4):
    lanes = ref.shape[1]
    size = rows_x * rows_y

    def rows(v, x, n):
        return ref[pl.ds(v * size + x * rows_y, n * rows_y), :].reshape(n, rows_y, lanes)

    step = min(step, rows_x)
    for x in range(0, rows_x, step):
        ws = [rows(v, x, step) for v in range(nv)]
        made = reaction(ws, act, *mixers)
        for v in range(nv):
            w = ws[v]
            first = rows(v, x - 1, 1) if x > 0 else low_edge(v)[None]
            last = rows(v, x + step, 1) if x + step < rows_x else high_edge(v)[None]
            beside = jnp.concatenate([first, w[:-1]], 0) + jnp.concatenate([w[1:], last], 0)
            lap = beside + shifted(w, 1) + shifted(w, 2) - 6.0 * w
            emit(v, x, step, w, dif[v] * lap + made[v])


def odd(axis):
    return lax.axis_index(axis) % 2 == 1


def two(one, other, is_odd, at):
    a, b = one[at, :], other[at, :]
    return jnp.where(is_odd, a, b), jnp.where(is_odd, b, a)


def far_side():
    return odd("gx")


def pack_x_kernel(dims, f_ref, q1, q2, low_ref, high_ref, sem):
    nv, rows_x, rows_y, _ = dims
    reads = [
        pltpu.make_async_copy(f_ref.at[:, pl.ds(0, 2)], low_ref, sem.at[0]),
        pltpu.make_async_copy(f_ref.at[:, pl.ds(rows_x - 2, 2)], high_ref, sem.at[1]),
    ]
    for read in reads:
        read.start()
    for read in reads:
        read.wait()
    is_odd = odd("gx")
    for layer in range(2):
        for v in range(nv):
            low, high = low_ref[v, layer], high_ref[v, 1 - layer]
            at = pl.ds((layer * nv + v) * rows_y, rows_y)
            q1[at, :] = jnp.where(is_odd, low, high)
            q2[at, :] = jnp.where(is_odd, high, low)


def pack_y_kernel(dims, f_ref, x1, p1, p2):
    nv, rows_x, rows_y, _ = dims
    size = rows_x * rows_y

    def put(at, low, high):
        p1[at, :] = jnp.where(odd("gy"), low, high)
        p2[at, :] = jnp.where(odd("gy"), high, low)

    for layer in range(2):
        for v in range(nv):
            low = f_ref[pl.ds(v * size + layer, rows_x, stride=rows_y), :]
            high = f_ref[pl.ds(v * size + rows_y - 1 - layer, rows_x, stride=rows_y), :]
            put(pl.ds((layer * nv + v) * rows_x, rows_x), low, high)
    low, high = [x1[pl.ds(y, nv, stride=rows_y), :] for y in (0, rows_y - 1)]
    put(pl.ds(2 * rows_x * nv, nv), low, high)


def first_kernel(dims, f_ref, bz_ref, bv_ref, mix_ref, dif, pre, act, *outs):
    s_ref, k_ref, t_ref, u_ref, n_ref, both_ref, low_ref = outs
    nv, rows_x, rows_y, lanes = dims
    size = rows_x * rows_y
    spot = place((nv, nv), 1)
    scaled = mix_ref[...]
    for u in range(nv):
        scaled = jnp.where(spot == u, scaled * pre[u], scaled)
    wide = (nv * 8, nv)
    spread = (place(wide, 0) // 8 == place(wide, 1)).astype(jnp.float32)
    full = jnp.dot(spread, scaled, precision=HIGH, preferred_element_type=jnp.float32)
    full = lax.dot_general(
        full, spread, (((1,), (1,)), ((), ())), precision=HIGH, preferred_element_type=jnp.float32
    )
    hi, lo = split(jnp.where(place(full.shape, 0) % 8 == place(full.shape, 1) % 8, full, 0.0))
    both = jnp.concatenate([hi, hi], axis=1)
    both_ref[...], low_ref[...] = both, lo

    def emit(v, x, n, w, t):
        s_ref[pl.ds(v * size + x * rows_y, n * rows_y), :] = (w + t).reshape(n * rows_y, lanes)

    def nothing(v):
        return jnp.zeros((rows_y, lanes), jnp.float32)

    stage(f_ref, nv, rows_x, rows_y, dif, act, (both, lo), emit, nothing, nothing)
    bz, bv = bz_ref[...], bv_ref[...]
    rank_z, rank_v = bz.shape[0], bv.shape[0]
    width, part = rank_z * rank_v, nv * rank_z
    pick_z = (place((rank_z, width), 1) % rank_z == place((rank_z, width), 0)).astype(jnp.float32)
    pick_v = (place((rank_v, width), 1) // rank_z == place((rank_v, width), 0)).astype(jnp.float32)
    first = (((0,), (0,)), ((), ()))
    wide_z = lax.dot_general(bz, pick_z, first, precision=HIGH, preferred_element_type=jnp.float32)
    wide_v = lax.dot_general(bv, pick_v, first, precision=HIGH, preferred_element_type=jnp.float32)
    for v in range(nv):
        product = wide_z * wide_v[v : v + 1, :]
        at = slice(v * lanes, (v + 1) * lanes)
        k_ref[0, at, :], k_ref[1, at, :] = split(product)
        t_ref[0, :, at], t_ref[1, :, at] = split(product.T)
    pick_u = (place((nv, part), 1) // rank_z == place((nv, part), 0)).astype(jnp.float32)
    tall = lax.dot_general(pick_v, bv, first, precision=HIGH, preferred_element_type=jnp.float32)
    tall = jnp.dot(tall, pick_u, precision=HIGH, preferred_element_type=jnp.float32)
    same = place((width, part), 0) % rank_z == place((width, part), 1) % rank_z
    u_ref[0], u_ref[1] = split(jnp.where(same, tall, 0.0))
    held = lanes // rank_z
    spread = (place((rank_z, lanes), 1) % rank_z == place((rank_z, lanes), 0)).astype(jnp.float32)
    wide_z = lax.dot_general(bz, spread, first, precision=HIGH, preferred_element_type=jnp.float32)
    group = place((lanes, lanes), 1) // rank_z
    for j in range(held):
        at = slice(j * lanes, (j + 1) * lanes)
        n_ref[0, at, :], n_ref[1, at, :] = split(jnp.where(group == j, wide_z, 0.0))


def second_kernel(
    dims, f_ref, s_ref, y1, y2, x1, x2, bx_ref, k_ref, both_ref, low_ref, dif, act,
    state_ref, m_ref, sec, gy_ref, gx_ref,
):
    nv, rows_x, rows_y, lanes = dims
    size = rows_x * rows_y
    ix, iy = lax.axis_index("gx"), lax.axis_index("gy")
    has_x = (ix > 0, ix < lax.axis_size("gx") - 1)
    has_y = (iy > 0, iy < lax.axis_size("gy") - 1)
    mixers = (both_ref[...], low_ref[...])

    def y_ghost(layer, v):
        return jnp.stack(two(y1, y2, odd("gy"), pl.ds((layer * nv + v) * rows_x, rows_x)))

    def x_ghost(layer, v):
        return jnp.stack(two(x1, x2, odd("gx"), pl.ds((layer * nv + v) * rows_y, rows_y)))

    far = far_side()

    def corners(v):
        near = two(y1, y2, odd("gy"), pl.ds(2 * rows_x * nv + v, 1))
        return [jnp.where(far, a, 0.0) for a in near], [jnp.where(far, 0.0, a) for a in near]

    def keep(value, flags):
        inside = [jnp.where(flags[i], value[i], 0.0) for i in range(2)]
        return jnp.concatenate(inside, axis=0)

    ys = [y_ghost(0, v) for v in range(nv)]
    xs = [x_ghost(0, v) for v in range(nv)]
    made = reaction([jnp.concatenate([tiles_of(ys[v]), tiles_of(xs[v])], 0) for v in range(nv)], act, *mixers)
    for v in range(nv):
        g = ys[v]
        cut = g.size // (8 * lanes)
        low = f_ref[pl.ds(v * size, rows_x, stride=rows_y), :]
        high = f_ref[pl.ds(v * size + rows_y - 1, rows_x, stride=rows_y), :]
        left, right = corners(v)
        lap = y_ghost(1, v) + jnp.stack([low, high]) - 6.0 * g
        lap = lap + shifted(g, 1, jnp.stack(left), jnp.stack(right)) + shifted(g, 2)
        out = g + (dif[v] * lap + made[v][:cut].reshape(g.shape))
        gy_ref[pl.ds(v * 2 * rows_x, 2 * rows_x), :] = keep(out, has_y)
        sec[pl.ds(v * size, size), :] = s_ref[pl.ds(v * size, size), :]
        at = pl.ds(v * size, rows_x, stride=rows_y)
        sec[at, :] = sec[at, :] + dif[v] * g[0]
        at = pl.ds(v * size + rows_y - 1, rows_x, stride=rows_y)
        sec[at, :] = sec[at, :] + dif[v] * g[1]
        g = xs[v]
        low = f_ref[pl.ds(v * size, rows_y), :]
        high = f_ref[pl.ds(v * size + size - rows_y, rows_y), :]
        before = jnp.stack([left[0], right[0]])
        after = jnp.stack([left[1], right[1]])
        lap = x_ghost(1, v) + jnp.stack([low, high]) - 6.0 * g
        lap = lap + shifted(g, 1, before, after) + shifted(g, 2)
        out = g + (dif[v] * lap + made[v][cut:].reshape(g.shape))
        gx_ref[pl.ds(v * 2 * rows_y, 2 * rows_y), :] = keep(out, has_x)
        at = pl.ds(v * size, rows_y)
        sec[at, :] = sec[at, :] + dif[v] * g[0]
        at = pl.ds(v * size + size - rows_y, rows_y)
        sec[at, :] = sec[at, :] + dif[v] * g[1]

    def emit(v, x, n, w, t):
        at = pl.ds(v * size + x * rows_y, n * rows_y)
        state_ref[at, :] = 0.5 * ((f_ref[at, :] + w.reshape(n * rows_y, lanes)) + t.reshape(n * rows_y, lanes))

    stage(
        sec, nv, rows_x, rows_y, dif, act, mixers, emit,
        lambda v: gx_ref[pl.ds(v * 2 * rows_y, rows_y), :],
        lambda v: gx_ref[pl.ds((v * 2 + 1) * rows_y, rows_y), :],
    )
    his, los = [], []
    edge = jnp.where(far, rows_x - 1, 0)
    for v in range(nv):
        half = 0.5 * dif[v]
        at = pl.ds(v * size, rows_x, stride=rows_y)
        state_ref[at, :] = state_ref[at, :] + half * gy_ref[pl.ds(v * 2 * rows_x, rows_x), :]
        at = pl.ds(v * size + rows_y - 1, rows_x, stride=rows_y)
        state_ref[at, :] = state_ref[at, :] + half * gy_ref[pl.ds((v * 2 + 1) * rows_x, rows_x), :]
        ends = [dif[v] * dif[v] * a for a in two(y1, y2, odd("gy"), pl.ds(v * rows_x + edge, 1))]
        for end in range(2):
            m_ref[pl.ds(spots(dims, k_ref.shape[2], bx_ref.shape[1])[2] + end * nv + v, 1), :] = ends[end]
        lack = jnp.concatenate([ends_tile(*ends, rows_y), jnp.zeros((-rows_y % 16, lanes), jnp.float32)], axis=0)
        hi, lo = split(jnp.concatenate([state_ref[pl.ds(v * size, size), :], lack], axis=0))
        his.append(hi)
        los.append(lo)
    total = mm3((jnp.concatenate(his, 1), jnp.concatenate(los, 1)), (k_ref[0], k_ref[1]))
    pack_message(dims, m_ref, total[:size], bx_ref[...], total[size : size + rows_y])


def ends_tile(first, last, rows):
    shape = (rows, first.shape[1])
    return jnp.where(place(shape, 0) == 0, first, jnp.where(place(shape, 0) == rows - 1, last, 0.0))


def spots(dims, width, rank_x):
    nv, rows_x, rows_y, lanes = dims
    size = rows_x * rows_y
    assert width % lanes * 2 == lanes and rank_x * 2 == lanes
    tail = width // lanes * size
    basis = tail + size // 2
    ends = basis + rows_x // 2
    made = ends + 2 * nv
    return tail, basis, ends, made, made + -(-(width // lanes * 2 + 1) // 8) * 8


def fold(a):
    half = a.shape[0] // 2
    return jnp.concatenate([a[:half], a[half:]], axis=1)


def unfold(a):
    half = a.shape[1] // 2
    return jnp.concatenate([a[:, :half], a[:, half:]], axis=0)


def pack_message(dims, m_ref, values, basis, ends):
    _, rows_x, rows_y, lanes = dims
    size, width = values.shape
    tail, base, _, made, _ = spots(dims, width, basis.shape[1])
    whole = width // lanes
    for i in range(whole):
        m_ref[pl.ds(i * size, size), :] = values[:, i * lanes : (i + 1) * lanes]
        for end, row in enumerate((0, rows_y - 1)):
            m_ref[pl.ds(made + 2 * i + end, 1), :] = ends[row : row + 1, i * lanes : (i + 1) * lanes]
    m_ref[pl.ds(tail, size // 2), :] = fold(values[:, whole * lanes :])
    m_ref[pl.ds(base, rows_x // 2), :] = fold(basis)
    rest = [ends[row : row + 1, whole * lanes :] for row in (0, rows_y - 1)]
    m_ref[pl.ds(made + 2 * whole, 1), :] = jnp.concatenate(rest, axis=1)


def unpack_message(dims, m_ref, width, rank_x):
    _, rows_x, rows_y, lanes = dims
    size = rows_x * rows_y
    tail, base, _, made, _ = spots(dims, width, rank_x)
    whole = width // lanes
    parts = [m_ref[pl.ds(i * size, size), :] for i in range(whole)]
    parts.append(unfold(m_ref[pl.ds(tail, size // 2), :]))
    basis = unfold(m_ref[pl.ds(base, rows_x // 2), :])
    rest = m_ref[pl.ds(made + 2 * whole, 1), :]
    half = lanes // 2
    ends = [
        jnp.concatenate(
            [m_ref[pl.ds(made + 2 * i + end, 1), :] for i in range(whole)] + [rest[:, end * half : (end + 1) * half]],
            axis=1,
        )
        for end in range(2)
    ]
    return jnp.concatenate(parts, axis=1), basis, ends_tile(*ends, rows_y)


def from_far(me, masks, index, items):
    block = jnp.bitwise_xor(me, masks[index])
    far = jnp.where(block % 2 == 1, block + 1, block - 1)
    total = None
    mask = 3
    while mask < len(masks):
        other = masks.index(masks[index] ^ mask)
        item = jnp.where(far == jnp.bitwise_xor(block, mask), items[other], 0.0)
        total = item if total is None else total + item
        mask = 2 * mask + 1
    return total


def mix_blocks(dims, width, rank_x, masks, refs):
    _, rows_x, rows_y, _ = dims
    size = rows_x * rows_y
    me = lax.axis_index("gx")

    def repeated(basis):
        return jnp.broadcast_to(basis[:, None, :], (rows_x, rows_y, rank_x)).reshape(size, rank_x)

    parts = [unpack_message(dims, ref, width, rank_x) for ref in refs]
    values = []
    for i, (value, _, _) in enumerate(parts):
        lack = from_far(me, masks, i, [ends for _, _, ends in parts])
        if lack is not None:
            last = jnp.bitwise_xor(me, masks[i]) % 2 == 1
            top = value[:rows_y] + jnp.where(last, 0.0, lack)
            bottom = value[size - rows_y :] + jnp.where(last, lack, 0.0)
            value = jnp.concatenate([top, value[rows_y : size - rows_y], bottom], axis=0)
        values.append(value)
    values = jnp.concatenate(values, axis=0)
    bases = jnp.concatenate([repeated(basis) for _, basis, _ in parts], axis=0)
    hi, lo = split(bases)
    link = mm3((hi[:size], lo[:size]), (hi, lo), True)
    same = place(link.shape, 0) % rows_y == place(link.shape, 1) % rows_y
    return mm3(split(jnp.where(same, link, 0.0)), split(values))


def squares(a):
    return jnp.sum((a * a).reshape(a.shape[0] // 8, 8, a.shape[1]), axis=0)


def zero_one(flags):
    return flags.astype(jnp.float32).astype(jnp.bfloat16)


def tally(outside, mass, lanes):
    hi, lo = split(jnp.concatenate(outside + mass, axis=0))
    ones = jnp.ones((8, lanes), jnp.bfloat16)
    hi, lo = split(mm(ones, hi, True) + mm(ones, lo, True))
    shape = (hi.shape[1], lanes)
    pick = zero_one(place(shape, 0) // 8 == place(shape, 1))
    return mm(hi, pick) + mm(lo, pick)


def outside_span(state, basis):
    coefs = mm3(split(state), basis)
    return coefs, state - mm3(split(coefs), basis, True)


def side_kernel(dims, rank_z, state_ref, n_ref, w_ref, row_ref):
    nv, rows_x, rows_y, lanes = dims
    size = rows_x * rows_y
    held = lanes // rank_z
    last = far_side()
    outside, mass = [], []
    for v in range(0, nv, held):
        state = jnp.concatenate([state_ref[pl.ds((v + j) * size, size), :] for j in range(held)], axis=1)
        top = jnp.where(last, state[:rows_y], 0.0)
        bottom = jnp.where(last, 0.0, state[size - rows_y :])
        state = jnp.concatenate([top, state[rows_y : size - rows_y], bottom], axis=0)
        coefs, rest = outside_span(state, (n_ref[0], n_ref[1]))
        w_ref[:, (v // held) * lanes : (v // held + 1) * lanes] = coefs
        for j in range(held):
            outside.append(squares(rest[:, j * lanes : (j + 1) * lanes]))
            mass.append(squares(state[:, j * lanes : (j + 1) * lanes]))
    row_ref[...] = tally(outside, mass, lanes)


def edge_rows(dims, rank_z, state_ref, lack_ref, n_ref):
    nv, rows_x, rows_y, lanes = dims
    size = rows_x * rows_y
    held = lanes // rank_z
    start = jnp.where(far_side(), size - rows_y, 0)
    whole = []
    for v in range(nv):
        at = pl.ds(pl.multiple_of(v * size + start, rows_y), rows_y)
        ends = [lack_ref[pl.ds(end * nv + v, 1), :] for end in range(2)]
        whole.append(state_ref[at, :] + ends_tile(*ends, rows_y))
    state = jnp.concatenate(
        [jnp.concatenate(whole[v : v + held], axis=1) for v in range(0, nv, held)], axis=0
    )
    coefs, rest = outside_span(state, (n_ref[0], n_ref[1]))
    outside = []
    for v in range(nv):
        i, j = divmod(v, held)
        outside.append(squares(rest[i * rows_y : (i + 1) * rows_y, j * lanes : (j + 1) * lanes]))
    row = tally(outside, [squares(a) for a in whole], lanes)
    coefs = jnp.concatenate([coefs[i * rows_y : (i + 1) * rows_y] for i in range(nv // held)], axis=1)
    return coefs, row


def settle(dims, rank_z, mixed, lack_ref, state_ref, n_ref, w_ref, row_ref, u_ref, sums_ref):
    _, _, rows_y, lanes = dims
    coefs, edge_row = edge_rows(dims, rank_z, state_ref, lack_ref, n_ref)
    last = far_side()
    w = w_ref[...]
    size, part = w.shape
    top = w[:rows_y] + jnp.where(last, 0.0, coefs)
    bottom = w[size - rows_y :] + jnp.where(last, coefs, 0.0)
    w = jnp.concatenate([top, w[rows_y : size - rows_y], bottom], axis=0)
    gap = w - mm3(split(mixed), (u_ref[0], u_ref[1]))
    hi, lo = split(squares(gap))
    shape = (part, lanes)
    pick = zero_one(place(shape, 0) // rank_z == place(shape, 1))
    row = jnp.sum(mm(hi, pick) + mm(lo, pick), axis=0, keepdims=True) + row_ref[0:1, :] + edge_row[0:1, :]
    sums_ref[...] = jnp.broadcast_to(row, sums_ref.shape)


def find_lack(dims, width, rank_x, masks, refs, lack_ref):
    spot = spots(dims, width, rank_x)[2]
    rows = [ref[pl.ds(spot, 2 * dims[0]), :] for ref in refs]
    lack = from_far(lax.axis_index("gx"), masks, 0, rows)
    lack_ref[...] = jnp.zeros(lack_ref.shape, jnp.float32) if lack is None else lack


def third_kernel(dims, rank_z, width, rank_x, masks, *refs):
    n = len(masks)
    state_ref, n_ref, w_ref, row_ref, u_ref, d_ref, lack_ref, sums_ref = refs[n:]
    find_lack(dims, width, rank_x, masks, refs[:n], lack_ref)
    mixed = mix_blocks(dims, width, rank_x, masks, refs[:n])
    d_ref[...] = mixed
    settle(dims, rank_z, mixed, lack_ref, state_ref, n_ref, w_ref, row_ref, u_ref, sums_ref)


def mix_kernel(dims, width, rank_x, masks, *refs):
    n = len(masks)
    find_lack(dims, width, rank_x, masks, refs[:n], refs[n + 1])
    refs[n][...] = mix_blocks(dims, width, rank_x, masks, refs[:n])


def settle_kernel(dims, rank_z, d_ref, lack_ref, state_ref, n_ref, w_ref, row_ref, u_ref, sums_ref):
    settle(dims, rank_z, d_ref[...], lack_ref, state_ref, n_ref, w_ref, row_ref, u_ref, sums_ref)


def decode_kernel(dims, d_ref, t_ref, lack_ref, state_ref, recon_ref, out_ref):
    nv, rows_x, rows_y, lanes = dims
    size = rows_x * rows_y
    halves = split(d_ref[...])
    start = jnp.where(far_side(), size - rows_y, 0)
    for v in range(nv):
        whole = pl.ds(v * size, size)
        out_ref[whole, :] = state_ref[whole, :]
        at = pl.ds(pl.multiple_of(v * size + start, rows_y), rows_y)
        ends = [lack_ref[pl.ds(end * nv + v, 1), :] for end in range(2)]
        out_ref[at, :] = state_ref[at, :] + ends_tile(*ends, rows_y)
        cols = slice(v * lanes, (v + 1) * lanes)
        recon_ref[whole, :] = mm3(halves, (t_ref[0, :, cols], t_ref[1, :, cols]))


def pairs(n, first):
    swaps = [(i, i + 1) for i in range(first, n - 1, 2)]
    return swaps + [(j, i) for i, j in swaps]


def gather_blocks(block):
    n = lax.axis_size("gx")
    assert n & (n - 1) == 0
    blocks, masks = [block], [0]
    bit = n // 2
    while bit:
        swaps = [(i, i ^ bit) for i in range(n)]
        blocks = blocks + [lax.ppermute(b, "gx", swaps) for b in blocks]
        masks = masks + [mask ^ bit for mask in masks]
        bit //= 2
    return blocks, tuple(masks)


def program(field, diffusion, prefactor, activation, mixing, basis_x, basis_y, basis_z, basis_v):
    f32, bf16 = jnp.float32, jnp.bfloat16
    dims = field.shape
    nv, rows_x, rows_y, lanes = dims
    size = rows_x * rows_y
    rank_x, rank_z, rank_v = basis_x.shape[1], basis_z.shape[1], basis_v.shape[1]
    width, part = rank_z * rank_v, nv * rank_z
    gx, gy = lax.axis_size("gx"), lax.axis_size("gy")
    peers = gx * gy
    flat = field.reshape(nv * size, lanes)
    block = (nv * size, lanes)

    y_msg, x_msg = (nv * (2 * rows_x + 1), lanes), (2 * nv * rows_y, lanes)
    edges = (nv, 2, rows_y, lanes)
    q1, q2 = call(
        functools.partial(pack_x_kernel, dims),
        [(x_msg, f32)] * 2,
        [pl.BlockSpec(memory_space=pltpu.HBM)],
        [pltpu.VMEM(edges, f32)] * 2 + [pltpu.SemaphoreType.DMA((2,))],
    )(field)
    x2 = lax.ppermute(q2, "gx", pairs(gx, 1))
    x1 = lax.ppermute(q1, "gx", pairs(gx, 0))
    p1, p2 = call(functools.partial(pack_y_kernel, dims), [(y_msg, f32)] * 2, [VM] * 2)(flat, x1)
    y1 = lax.ppermute(p1, "gy", pairs(gy, 0))
    y2 = lax.ppermute(p2, "gy", pairs(gy, 1))

    section, k, t, u, n, both, low = call(
        functools.partial(first_kernel, dims),
        [
            (block, f32),
            ((2, nv * lanes, width), bf16),
            ((2, width, nv * lanes), bf16),
            ((2, width, part), bf16),
            ((2, lanes // rank_z * lanes, lanes), bf16),
            ((nv * 8, nv * 16), bf16),
            ((nv * 8, nv * 8), bf16),
        ],
        [VM] * 4 + [SM] * 3,
    )(flat, basis_z.T, basis_v.T, mixing, diffusion, prefactor, activation)
    state, message = call(
        functools.partial(second_kernel, dims),
        [(block, f32), ((spots(dims, width, rank_x)[4], lanes), f32)],
        [VM] * 10 + [SM] * 2,
        [
            pltpu.VMEM(block, f32),
            pltpu.VMEM((nv * 2 * rows_x, lanes), f32),
            pltpu.VMEM((nv * 2 * rows_y, lanes), f32),
        ],
    )(flat, section, y1, y2, x1, x2, basis_x, k, both, low, diffusion, activation)
    blocks, masks = gather_blocks(message)
    count = len(blocks)
    coefs, row = call(
        functools.partial(side_kernel, dims, rank_z), [((size, part), f32), ((8, lanes), f32)], [VM] * 2
    )(state, n)
    outs = [((size, width), f32), ((2 * nv, lanes), f32), ((peers, lanes), f32)]
    mixing_args = (width, rank_x, masks)
    rest = (state, n, coefs, row, u)
    if basis_y.shape[0] * gy == basis_y.shape[1]:
        mixed, lack, sums = call(
            functools.partial(third_kernel, dims, rank_z, *mixing_args), outs, [VM] * (count + 5)
        )(*blocks, *rest)
    else:
        mixed, lack = call(functools.partial(mix_kernel, dims, *mixing_args), outs[:2], [VM] * count)(*blocks)
        mixed = mixed.reshape(rows_x, rows_y, width)
        core = lax.psum(jnp.einsum("xyk,yb->xbk", mixed, basis_y, precision=HIGH), "gy")
        mixed = jnp.einsum("xbk,yb->xyk", core, basis_y, precision=HIGH).reshape(size, width)
        (sums,) = call(functools.partial(settle_kernel, dims, rank_z), outs[2:], [VM] * 7)(
            mixed, lack, *rest
        )
    recon, state = call(functools.partial(decode_kernel, dims), [(block, f32)] * 2, [VM] * 4)(mixed, t, lack, state)
    if peers > 64:
        sums = lax.psum(sums[0], ("gx", "gy"))
    else:
        sums = jnp.sum(lax.all_to_all(sums, ("gx", "gy"), 0, 0, tiled=True), axis=0)
    residual = jnp.sqrt(sums[:nv] / (sums[nv : 2 * nv] + 1e-06))
    return (state.reshape(dims), recon.reshape(dims), residual)


def solution(mesh):
    return jax.shard_map(
        program,
        mesh=mesh,
        in_specs=(
            P(None, "gx", "gy", None),
            P(),
            P(),
            P(),
            P(),
            P("gx", None),
            P("gy", None),
            P(),
            P(),
        ),
        out_specs=(P(None, "gx", "gy", None), P(None, "gx", "gy", None), P()),
        check_vma=False,
    )
```

```python
import functools

import jax
import jax.numpy as jnp
from jax import lax
from jax.experimental import pallas as pl
from jax.experimental.pallas import tpu as pltpu
from jax.sharding import PartitionSpec as P


HIGH = lax.Precision.HIGHEST
VM = pl.BlockSpec(memory_space=pltpu.VMEM)
SM = pl.BlockSpec(memory_space=pltpu.SMEM)


def call(kernel, outs, in_specs, scratch=(), vmem=12, out_specs=None):
    return pl.pallas_call(
        kernel,
        out_shape=[jax.ShapeDtypeStruct(s, d) for s, d in outs],
        in_specs=in_specs,
        out_specs=out_specs or [VM] * len(outs),
        scratch_shapes=list(scratch),
        compiler_params=pltpu.CompilerParams(vmem_limit_bytes=vmem << 20),
        cost_estimate=pl.CostEstimate(flops=10**7, bytes_accessed=10**6, transcendentals=0),
    )


def split(a):
    hi = a.astype(jnp.bfloat16)
    lo = (a - hi.astype(jnp.float32)).astype(jnp.bfloat16)
    return hi, lo


def mm(a, b, nt=False):
    dims = (((1,), (1 if nt else 0,)), ((), ()))
    return lax.dot_general(a, b, dims, preferred_element_type=jnp.float32)


def mm3(a, b, nt=False):
    return mm(a[0], b[0], nt) + mm(a[0], b[1], nt) + mm(a[1], b[0], nt)


def place(shape, dim):
    return lax.broadcasted_iota(jnp.int32, shape, dim)


def shifted(w, axis, before=0.0, after=0.0):
    size = w.shape[axis]
    pos = place(w.shape, axis)
    low = jnp.where(pos == 0, before, pltpu.roll(w, 1, axis))
    high = jnp.where(pos == size - 1, after, pltpu.roll(w, size - 1, axis))
    return low + high


def tiles_of(a):
    return a.reshape(a.size // (8 * a.shape[-1]), 8, a.shape[-1])


def reaction(ws, act, both, low):
    n = len(ws)
    cold = -1.0 / (1.5 + jnp.tanh(ws[0]))
    rates = [tiles_of(jnp.exp(act[v] * cold) * ws[v]) for v in range(n)]
    count, lanes = rates[0].shape[0], rates[0].shape[2]
    stacked = jnp.concatenate(
        [jnp.concatenate([rates[v][t] for v in range(n)], axis=0) for t in range(count)], axis=1
    )
    hi, lo = split(stacked)
    out = mm(both, jnp.concatenate([hi, lo], axis=0)) + mm(low, hi)
    return [
        jnp.stack([out[v * 8 : (v + 1) * 8, t * lanes : (t + 1) * lanes] for t in range(count)]).reshape(ws[v].shape)
        for v in range(n)
    ]


def stage(ref, nv, rows_x, rows_y, dif, act, mixers, emit, low_edge, high_edge, step=4):
    lanes = ref.shape[1]
    size = rows_x * rows_y

    def rows(v, x, n):
        return ref[pl.ds(v * size + x * rows_y, n * rows_y), :].reshape(n, rows_y, lanes)

    step = min(step, rows_x)
    for x in range(0, rows_x, step):
        ws = [rows(v, x, step) for v in range(nv)]
        made = reaction(ws, act, *mixers)
        for v in range(nv):
            w = ws[v]
            first = rows(v, x - 1, 1) if x > 0 else low_edge(v)[None]
            last = rows(v, x + step, 1) if x + step < rows_x else high_edge(v)[None]
            beside = jnp.concatenate([first, w[:-1]], 0) + jnp.concatenate([w[1:], last], 0)
            lap = beside + shifted(w, 1) + shifted(w, 2) - 6.0 * w
            emit(v, x, step, w, dif[v] * lap + made[v])


def odd(axis):
    return lax.axis_index(axis) % 2 == 1


def two(one, other, is_odd, at):
    a, b = one[at, :], other[at, :]
    return jnp.where(is_odd, a, b), jnp.where(is_odd, b, a)


def far_side():
    return odd("gx")


def pack_y_kernel(dims, f_ref, p1, p2):
    nv, rows_x, rows_y, _ = dims
    size = rows_x * rows_y
    for layer in range(2):
        for v in range(nv):
            low = f_ref[pl.ds(v * size + layer, rows_x, stride=rows_y), :]
            high = f_ref[pl.ds(v * size + rows_y - 1 - layer, rows_x, stride=rows_y), :]
            at = pl.ds((layer * nv + v) * rows_x, rows_x)
            p1[at, :] = jnp.where(odd("gy"), low, high)
            p2[at, :] = jnp.where(odd("gy"), high, low)


def pack_x_kernel(dims, f_ref, q1, q2):
    nv, rows_x, rows_y, _ = dims
    size = rows_x * rows_y
    for layer in range(2):
        for v in range(nv):
            low = f_ref[pl.ds(v * size + layer * rows_y, rows_y), :]
            high = f_ref[pl.ds(v * size + (rows_x - 1 - layer) * rows_y, rows_y), :]
            at = pl.ds((layer * nv + v) * rows_y, rows_y)
            q1[at, :] = jnp.where(odd("gx"), low, high)
            q2[at, :] = jnp.where(odd("gx"), high, low)


def first_kernel(dims, f_ref, x1, bz_ref, bv_ref, mix_ref, dif, pre, act, *outs):
    s_ref, k_ref, t_ref, u_ref, n_ref, both_ref, low_ref = outs
    nv, rows_x, rows_y, lanes = dims
    size = rows_x * rows_y
    spot = place((nv, nv), 1)
    scaled = mix_ref[...]
    for u in range(nv):
        scaled = jnp.where(spot == u, scaled * pre[u], scaled)
    wide = (nv * 8, nv)
    spread = (place(wide, 0) // 8 == place(wide, 1)).astype(jnp.float32)
    full = jnp.dot(spread, scaled, precision=HIGH, preferred_element_type=jnp.float32)
    full = lax.dot_general(
        full, spread, (((1,), (1,)), ((), ())), precision=HIGH, preferred_element_type=jnp.float32
    )
    hi, lo = split(jnp.where(place(full.shape, 0) % 8 == place(full.shape, 1) % 8, full, 0.0))
    both = jnp.concatenate([hi, hi], axis=1)
    both_ref[...], low_ref[...] = both, lo

    def emit(v, x, n, w, t):
        s_ref[pl.ds(v * size + x * rows_y, n * rows_y), :] = (w + t).reshape(n * rows_y, lanes)

    def near(is_low):
        is_near = odd("gx") if is_low else jnp.logical_not(odd("gx"))
        return lambda v: jnp.where(is_near, x1[pl.ds(v * rows_y, rows_y), :], 0.0)

    stage(f_ref, nv, rows_x, rows_y, dif, act, (both, lo), emit, near(True), near(False))
    bz, bv = bz_ref[...], bv_ref[...]
    rank_z, rank_v = bz.shape[0], bv.shape[0]
    width, part = rank_z * rank_v, nv * rank_z
    pick_z = (place((rank_z, width), 1) % rank_z == place((rank_z, width), 0)).astype(jnp.float32)
    pick_v = (place((rank_v, width), 1) // rank_z == place((rank_v, width), 0)).astype(jnp.float32)
    first = (((0,), (0,)), ((), ()))
    wide_z = lax.dot_general(bz, pick_z, first, precision=HIGH, preferred_element_type=jnp.float32)
    wide_v = lax.dot_general(bv, pick_v, first, precision=HIGH, preferred_element_type=jnp.float32)
    for v in range(nv):
        product = wide_z * wide_v[v : v + 1, :]
        at = slice(v * lanes, (v + 1) * lanes)
        k_ref[0, at, :], k_ref[1, at, :] = split(product)
        t_ref[0, :, at], t_ref[1, :, at] = split(product.T)
    pick_u = (place((nv, part), 1) // rank_z == place((nv, part), 0)).astype(jnp.float32)
    tall = lax.dot_general(pick_v, bv, first, precision=HIGH, preferred_element_type=jnp.float32)
    tall = jnp.dot(tall, pick_u, precision=HIGH, preferred_element_type=jnp.float32)
    same = place((width, part), 0) % rank_z == place((width, part), 1) % rank_z
    u_ref[0], u_ref[1] = split(jnp.where(same, tall, 0.0))
    held = lanes // rank_z
    spread = (place((rank_z, lanes), 1) % rank_z == place((rank_z, lanes), 0)).astype(jnp.float32)
    wide_z = lax.dot_general(bz, spread, first, precision=HIGH, preferred_element_type=jnp.float32)
    group = place((lanes, lanes), 1) // rank_z
    for j in range(held):
        at = slice(j * lanes, (j + 1) * lanes)
        n_ref[0, at, :], n_ref[1, at, :] = split(jnp.where(group == j, wide_z, 0.0))


def second_kernel(
    dims, f_ref, s_ref, y1, y2, x1, x2, bx_ref, k_ref, both_ref, low_ref, dif, act,
    state_ref, m_ref, near_ref, sec, gy_ref, gx_ref,
):
    nv, rows_x, rows_y, lanes = dims
    size = rows_x * rows_y
    ix, iy = lax.axis_index("gx"), lax.axis_index("gy")
    has_x = (ix > 0, ix < lax.axis_size("gx") - 1)
    has_y = (iy > 0, iy < lax.axis_size("gy") - 1)
    mixers = (both_ref[...], low_ref[...])

    def y_ghost(layer, v):
        return jnp.stack(two(y1, y2, odd("gy"), pl.ds((layer * nv + v) * rows_x, rows_x)))

    def x_ghost(layer, v):
        return jnp.stack(two(x1, x2, odd("gx"), pl.ds((layer * nv + v) * rows_y, rows_y)))

    far = far_side()
    edges = (jnp.where(far, rows_x - 1, 0), jnp.where(far, 0, rows_x - 1))

    def keep(value, flags):
        inside = [jnp.where(flags[i], value[i], 0.0) for i in range(2)]
        return jnp.concatenate(inside, axis=0)

    ys = [y_ghost(0, v) for v in range(nv)]
    xs = [x_ghost(0, v) for v in range(nv)]
    made = reaction([jnp.concatenate([tiles_of(ys[v]), tiles_of(xs[v])], 0) for v in range(nv)], act, *mixers)
    for v in range(nv):
        g = ys[v]
        cut = g.size // (8 * lanes)
        low = f_ref[pl.ds(v * size, rows_x, stride=rows_y), :]
        high = f_ref[pl.ds(v * size + rows_y - 1, rows_x, stride=rows_y), :]
        lap = y_ghost(1, v) + jnp.stack([low, high]) - 6.0 * g
        lap = lap + shifted(g, 1) + shifted(g, 2)
        out = g + (dif[v] * lap + made[v][:cut].reshape(g.shape))
        gy_ref[pl.ds(v * 2 * rows_x, 2 * rows_x), :] = keep(out, has_y)
        sec[pl.ds(v * size, size), :] = s_ref[pl.ds(v * size, size), :]
        at = pl.ds(v * size, rows_x, stride=rows_y)
        sec[at, :] = sec[at, :] + dif[v] * g[0]
        at = pl.ds(v * size + rows_y - 1, rows_x, stride=rows_y)
        sec[at, :] = sec[at, :] + dif[v] * g[1]
        g = xs[v]
        low = f_ref[pl.ds(v * size, rows_y), :]
        high = f_ref[pl.ds(v * size + size - rows_y, rows_y), :]
        lap = x_ghost(1, v) + jnp.stack([low, high]) - 6.0 * g
        lap = lap + shifted(g, 1) + shifted(g, 2)
        out = g + (dif[v] * lap + made[v][cut:].reshape(g.shape))
        gx_ref[pl.ds(v * 2 * rows_y, 2 * rows_y), :] = keep(out, has_x)
        at = pl.ds(pl.multiple_of(v * size + edges[0] * rows_y, rows_y), rows_y)
        sec[at, :] = sec[at, :] + dif[v] * x2[pl.ds(v * rows_y, rows_y), :]

    def emit(v, x, n, w, t):
        at = pl.ds(v * size + x * rows_y, n * rows_y)
        state_ref[at, :] = 0.5 * ((f_ref[at, :] + w.reshape(n * rows_y, lanes)) + t.reshape(n * rows_y, lanes))

    stage(
        sec, nv, rows_x, rows_y, dif, act, mixers, emit,
        lambda v: gx_ref[pl.ds(v * 2 * rows_y, rows_y), :],
        lambda v: gx_ref[pl.ds((v * 2 + 1) * rows_y, rows_y), :],
    )
    his, los = [], []
    spot = spots(dims, k_ref.shape[2], bx_ref.shape[1])[2]
    for v in range(nv):
        half = 0.5 * dif[v]
        at = pl.ds(v * size, rows_x, stride=rows_y)
        state_ref[at, :] = state_ref[at, :] + half * gy_ref[pl.ds(v * 2 * rows_x, rows_x), :]
        at = pl.ds(v * size + rows_y - 1, rows_x, stride=rows_y)
        state_ref[at, :] = state_ref[at, :] + half * gy_ref[pl.ds((v * 2 + 1) * rows_x, rows_x), :]
        rows = [state_ref[pl.ds(v * size, size), :]]
        for out, start, edge in ((m_ref, spot, edges[0]), (near_ref, 0, edges[1])):
            ends = [dif[v] * dif[v] * a for a in two(y1, y2, odd("gy"), pl.ds(v * rows_x + edge, 1))]
            for end in range(2):
                out[pl.ds(start + end * nv + v, 1), :] = ends[end]
            rows.append(ends_tile(*ends, rows_y))
        hi, lo = split(jnp.concatenate(rows, axis=0))
        his.append(hi)
        los.append(lo)
    total = mm3((jnp.concatenate(his, 1), jnp.concatenate(los, 1)), (k_ref[0], k_ref[1]))
    pack_message(dims, m_ref, total[:size], bx_ref[...], total[size:])


def ends_tile(first, last, rows):
    shape = (rows, first.shape[1])
    return jnp.where(place(shape, 0) == 0, first, jnp.where(place(shape, 0) == rows - 1, last, 0.0))


def spots(dims, width, rank_x):
    nv, rows_x, rows_y, lanes = dims
    size = rows_x * rows_y
    assert width % lanes * 2 == lanes and rank_x * 2 == lanes
    tail = width // lanes * size
    basis = tail + size // 2
    ends = basis + rows_x // 2
    made = ends + 2 * nv
    return tail, basis, ends, made, made + -(-(width // lanes * 4 + 2) // 8) * 8


def fold(a):
    half = a.shape[0] // 2
    return jnp.concatenate([a[:half], a[half:]], axis=1)


def unfold(a):
    half = a.shape[1] // 2
    return jnp.concatenate([a[:, :half], a[:, half:]], axis=0)


def pack_message(dims, m_ref, values, basis, ends):
    _, rows_x, rows_y, lanes = dims
    size, width = values.shape
    tail, base, _, made, _ = spots(dims, width, basis.shape[1])
    whole = width // lanes
    ends = [ends[row : row + 1] for row in (0, rows_y - 1, rows_y, 2 * rows_y - 1)]
    for i in range(whole):
        m_ref[pl.ds(i * size, size), :] = values[:, i * lanes : (i + 1) * lanes]
        for end in range(4):
            m_ref[pl.ds(made + 4 * i + end, 1), :] = ends[end][:, i * lanes : (i + 1) * lanes]
    m_ref[pl.ds(tail, size // 2), :] = fold(values[:, whole * lanes :])
    m_ref[pl.ds(base, rows_x // 2), :] = fold(basis)
    for end in range(0, 4, 2):
        rest = [ends[end][:, whole * lanes :], ends[end + 1][:, whole * lanes :]]
        m_ref[pl.ds(made + 4 * whole + end // 2, 1), :] = jnp.concatenate(rest, axis=1)


def unpack_message(dims, m_ref, width, rank_x):
    _, rows_x, rows_y, lanes = dims
    size = rows_x * rows_y
    tail, base, _, made, _ = spots(dims, width, rank_x)
    whole = width // lanes
    parts = [m_ref[pl.ds(i * size, size), :] for i in range(whole)]
    parts.append(unfold(m_ref[pl.ds(tail, size // 2), :]))
    basis = unfold(m_ref[pl.ds(base, rows_x // 2), :])
    half = lanes // 2
    ends = []
    for end in range(4):
        rest = m_ref[pl.ds(made + 4 * whole + end // 2, 1), :]
        rest = rest[:, end % 2 * half : (end % 2 + 1) * half]
        ends.append(jnp.concatenate([m_ref[pl.ds(made + 4 * i + end, 1), :] for i in range(whole)] + [rest], axis=1))
    tiles = ends_tile(*ends[:2], rows_y), ends_tile(*ends[2:], rows_y)
    return jnp.concatenate(parts, axis=1), basis, tiles


def from_far(me, masks, index, items):
    block = jnp.bitwise_xor(me, masks[index])
    far = jnp.where(block % 2 == 1, block + 1, block - 1)
    total = None
    mask = 3
    while mask < len(masks):
        other = masks.index(masks[index] ^ mask)
        item = jnp.where(far == jnp.bitwise_xor(block, mask), items[other], 0.0)
        total = item if total is None else total + item
        mask = 2 * mask + 1
    return total


def repeated(basis, rows_y):
    rows_x, rank_x = basis.shape
    return jnp.broadcast_to(basis[:, None, :], (rows_x, rows_y, rank_x)).reshape(rows_x * rows_y, rank_x)


def link_to(own, bases, rows_y):
    link = mm3(split(own), split(bases), True)
    return split(jnp.where(same_row(link, rows_y), link, 0.0))


def same_row(link, rows_y):
    return place(link.shape, 0) % rows_y == place(link.shape, 1) % rows_y


def mix_blocks(dims, width, rank_x, own_ref, refs):
    rows_y = dims[2]
    own = repeated(unpack_message(dims, own_ref, width, rank_x)[1], rows_y)
    parts = [unpack_message(dims, ref, width, rank_x) for ref in refs]
    values = jnp.concatenate([values for values, _, _ in parts], axis=0)
    bases = jnp.concatenate([repeated(basis, rows_y) for _, basis, _ in parts], axis=0)
    return mm3(link_to(own, bases, rows_y), split(values))


def premix_kernel(dims, width, rank_x, n, own_ref, *refs):
    refs[n][...] = mix_blocks(dims, width, rank_x, own_ref, refs[:n])


def second_premix_kernel(dims, width, rank_x, n, own_ref, *refs):
    d_ref, w_ref, u_ref, out_ref, gap_ref = refs[n:]
    mixed = d_ref[...] + mix_blocks(dims, width, rank_x, own_ref, refs[:n])
    out_ref[...] = mixed
    gap_ref[...] = w_ref[...] - mm3(split(mixed), (u_ref[0], u_ref[1]))


def last_values(dims, width, rank_x, masks, refs):
    _, rows_x, rows_y, _ = dims
    me = lax.axis_index("gx")
    parts = [unpack_message(dims, ref, width, rank_x) for ref in refs]
    values, bases = [parts[-1][0]], [repeated(parts[-1][1], rows_y)]
    for i, (_, basis, _) in enumerate(parts):
        last = jnp.bitwise_xor(me, masks[i]) % 2 == 1
        near = parts[masks.index(masks[i] ^ 1)][2][1]
        lacks = (from_far(me, masks, i, [ends[0] for _, _, ends in parts]), near)
        rows = (jnp.where(last, basis[rows_x - 1 :], basis[:1]), jnp.where(last, basis[:1], basis[rows_x - 1 :]))
        for lack, row in zip(lacks, rows):
            if lack is not None:
                values.append(lack)
                bases.append(jnp.broadcast_to(row, (rows_y, rank_x)))
    own = repeated(parts[0][1], rows_y)
    return split(jnp.concatenate(values, axis=0)), own, jnp.concatenate(bases, axis=0)


def squares(a):
    return jnp.sum((a * a).reshape(a.shape[0] // 8, 8, a.shape[1]), axis=0)


def zero_one(flags):
    return flags.astype(jnp.float32).astype(jnp.bfloat16)


def tally(outside, mass, lanes):
    hi, lo = split(jnp.concatenate(outside + mass, axis=0))
    ones = jnp.ones((8, lanes), jnp.bfloat16)
    hi, lo = split(mm(ones, hi, True) + mm(ones, lo, True))
    shape = (hi.shape[1], lanes)
    pick = zero_one(place(shape, 0) // 8 == place(shape, 1))
    return mm(hi, pick) + mm(lo, pick)


def outside_span(state, basis):
    coefs = mm3(split(state), basis)
    return coefs, state - mm3(split(coefs), basis, True)


def tile_of(ref, nv, v, rows_y):
    return ends_tile(ref[pl.ds(v, 1), :], ref[pl.ds(nv + v, 1), :], rows_y)


def side_kernel(dims, rank_z, state_ref, near_ref, n_ref, w_ref, row_ref):
    nv, rows_x, rows_y, lanes = dims
    size = rows_x * rows_y
    held = lanes // rank_z
    last = far_side()
    outside, mass = [], []
    for v in range(0, nv, held):
        state = jnp.concatenate([state_ref[pl.ds((v + j) * size, size), :] for j in range(held)], axis=1)
        near = jnp.concatenate([tile_of(near_ref, nv, v + j, rows_y) for j in range(held)], axis=1)
        top = jnp.where(last, state[:rows_y] + near, 0.0)
        bottom = jnp.where(last, 0.0, state[size - rows_y :] + near)
        state = jnp.concatenate([top, state[rows_y : size - rows_y], bottom], axis=0)
        coefs, rest = outside_span(state, (n_ref[0], n_ref[1]))
        w_ref[:, (v // held) * lanes : (v // held + 1) * lanes] = coefs
        for j in range(held):
            outside.append(squares(rest[:, j * lanes : (j + 1) * lanes]))
            mass.append(squares(state[:, j * lanes : (j + 1) * lanes]))
    row_ref[...] = tally(outside, mass, lanes)


def edge_state(dims, rank_z, state_ref, lack):
    nv, rows_x, rows_y, lanes = dims
    start = jnp.where(far_side(), (rows_x - 1) * rows_y, 0)
    held = lanes // rank_z
    whole = []
    for v in range(nv):
        at = pl.ds(pl.multiple_of(v * rows_x * rows_y + start, rows_y), rows_y)
        ends = [lack[end * nv + v : end * nv + v + 1] for end in range(2)]
        whole.append(state_ref[at, :] + ends_tile(*ends, rows_y))
    packed = [jnp.concatenate(whole[v : v + held], axis=1) for v in range(0, nv, held)]
    return whole, jnp.concatenate(packed, axis=0)


def edge_sums(dims, rank_z, whole, rest):
    nv, _, rows_y, lanes = dims
    held = lanes // rank_z
    outside = []
    for v in range(nv):
        i, j = divmod(v, held)
        outside.append(squares(rest[i * rows_y : (i + 1) * rows_y, j * lanes : (j + 1) * lanes]))
    return tally(outside, [squares(a) for a in whole], lanes)[0:1, :]


def edge_coefs(rows_y, coefs):
    count = coefs.shape[0] // rows_y
    return jnp.concatenate([coefs[i * rows_y : (i + 1) * rows_y] for i in range(count)], axis=1)


def put_edge(w, coefs):
    rows_y, last = coefs.shape[0], far_side()
    size = w.shape[0]
    top = w[:rows_y] + jnp.where(last, 0.0, coefs)
    bottom = w[size - rows_y :] + jnp.where(last, coefs, 0.0)
    return jnp.concatenate([top, w[rows_y : size - rows_y], bottom], axis=0)


def total_sums(gap, rows, sums_ref, rank_z):
    hi, lo = split(squares(gap))
    shape = (gap.shape[1], sums_ref.shape[1])
    pick = zero_one(place(shape, 0) // rank_z == place(shape, 1))
    row = jnp.sum(mm(hi, pick) + mm(lo, pick), axis=0, keepdims=True) + rows[0] + rows[1]
    sums_ref[...] = jnp.broadcast_to(row, sums_ref.shape)


def find_lack(dims, width, rank_x, masks, refs):
    spot = spots(dims, width, rank_x)[2]
    rows = [ref[pl.ds(spot, 2 * dims[0]), :] for ref in refs]
    lack = from_far(lax.axis_index("gx"), masks, 0, rows)
    return jnp.zeros_like(rows[0]) if lack is None else lack


def third_kernel(dims, rank_z, width, rank_x, masks, *refs):
    n = len(masks)
    state_ref, n_ref, row_ref, u_ref, part_ref, gap_ref, d_ref, lack_ref, sums_ref = refs[n:]
    rows_y = dims[2]
    values, own, bases = last_values(dims, width, rank_x, masks, refs[:n])
    lack = find_lack(dims, width, rank_x, masks, refs[:n])
    whole, edge = edge_state(dims, rank_z, state_ref, lack)
    basis = (n_ref[0], n_ref[1])
    link = mm3(split(own), split(bases), True)
    coefs = mm3(split(edge), basis)
    spread = mm3(values, (u_ref[0], u_ref[1]))
    link = split(jnp.where(same_row(link, rows_y), link, 0.0))
    rest = edge - mm3(split(coefs), basis, True)
    gap = mm3(link, split(spread))
    row = edge_sums(dims, rank_z, whole, rest)
    gap = put_edge(gap_ref[...], edge_coefs(rows_y, coefs)) - gap
    total_sums(gap, (row_ref[0:1, :], row), sums_ref, rank_z)
    lack_ref[...] = lack
    d_ref[...] = part_ref[...] + mm3(link, values)


def mix_kernel(dims, width, rank_x, masks, *refs):
    n = len(masks)
    part_ref, d_ref, lack_ref = refs[n:]
    lack_ref[...] = find_lack(dims, width, rank_x, masks, refs[:n])
    values, own, bases = last_values(dims, width, rank_x, masks, refs[:n])
    d_ref[...] = part_ref[...] + mm3(link_to(own, bases, dims[2]), values)


def settle_kernel(dims, rank_z, d_ref, lack_ref, state_ref, n_ref, row_ref, u_ref, w_ref, sums_ref):
    whole, edge = edge_state(dims, rank_z, state_ref, lack_ref[...])
    coefs, rest = outside_span(edge, (n_ref[0], n_ref[1]))
    row = edge_sums(dims, rank_z, whole, rest)
    gap = put_edge(w_ref[...], edge_coefs(dims[2], coefs)) - mm3(split(d_ref[...]), (u_ref[0], u_ref[1]))
    total_sums(gap, (row_ref[0:1, :], row), sums_ref, rank_z)


def decode_kernel(dims, d_ref, t_ref, lack_ref, near_ref, state_ref, recon_ref, out_ref):
    nv, rows_x, rows_y, lanes = dims
    size = rows_x * rows_y
    halves = split(d_ref[...])
    far = far_side()
    starts = (jnp.where(far, size - rows_y, 0), jnp.where(far, 0, size - rows_y))
    for v in range(nv):
        whole = pl.ds(v * size, size)
        out_ref[whole, :] = state_ref[whole, :]
        for start, ref in zip(starts, (lack_ref, near_ref)):
            at = pl.ds(pl.multiple_of(v * size + start, rows_y), rows_y)
            out_ref[at, :] = state_ref[at, :] + tile_of(ref, nv, v, rows_y)
        cols = slice(v * lanes, (v + 1) * lanes)
        recon_ref[whole, :] = mm3(halves, (t_ref[0, :, cols], t_ref[1, :, cols]))


def pairs(n, first):
    swaps = [(i, i + 1) for i in range(first, n - 1, 2)]
    return swaps + [(j, i) for i, j in swaps]


def gather_blocks(block):
    n = lax.axis_size("gx")
    assert n & (n - 1) == 0
    blocks, masks = [block], [0]
    bit = n // 2
    while bit:
        swaps = [(i, i ^ bit) for i in range(n)]
        blocks = blocks + [lax.ppermute(b, "gx", swaps) for b in blocks]
        masks = masks + [mask ^ bit for mask in masks]
        bit //= 2
    return blocks, tuple(masks)


def program(field, diffusion, prefactor, activation, mixing, basis_x, basis_y, basis_z, basis_v):
    f32, bf16 = jnp.float32, jnp.bfloat16
    dims = field.shape
    nv, rows_x, rows_y, lanes = dims
    size = rows_x * rows_y
    rank_x, rank_z, rank_v = basis_x.shape[1], basis_z.shape[1], basis_v.shape[1]
    width, part = rank_z * rank_v, nv * rank_z
    gx, gy = lax.axis_size("gx"), lax.axis_size("gy")
    peers = gx * gy
    flat = field.reshape(nv * size, lanes)
    block = (nv * size, lanes)

    y_msg, x_msg = (2 * nv * rows_x, lanes), (2 * nv * rows_y, lanes)
    p1, p2 = call(functools.partial(pack_y_kernel, dims), [(y_msg, f32)] * 2, [VM])(flat)
    y1 = lax.ppermute(p1, "gy", pairs(gy, 0))
    y2 = lax.ppermute(p2, "gy", pairs(gy, 1))
    q1, q2 = call(functools.partial(pack_x_kernel, dims), [(x_msg, f32)] * 2, [VM])(flat)
    x2 = lax.ppermute(q2, "gx", pairs(gx, 1))
    x1 = lax.ppermute(q1, "gx", pairs(gx, 0))

    section, k, t, u, n, both, low = call(
        functools.partial(first_kernel, dims),
        [
            (block, f32),
            ((2, nv * lanes, width), bf16),
            ((2, width, nv * lanes), bf16),
            ((2, width, part), bf16),
            ((2, lanes // rank_z * lanes, lanes), bf16),
            ((nv * 8, nv * 16), bf16),
            ((nv * 8, nv * 8), bf16),
        ],
        [VM] * 5 + [SM] * 3,
    )(flat, x1, basis_z.T, basis_v.T, mixing, diffusion, prefactor, activation)
    state, message, near = call(
        functools.partial(second_kernel, dims),
        [(block, f32), ((spots(dims, width, rank_x)[4], lanes), f32), ((2 * nv, lanes), f32)],
        [VM] * 10 + [SM] * 2,
        [
            pltpu.VMEM(block, f32),
            pltpu.VMEM((nv * 2 * rows_x, lanes), f32),
            pltpu.VMEM((nv * 2 * rows_y, lanes), f32),
        ],
    )(flat, section, y1, y2, x1, x2, basis_x, k, both, low, diffusion, activation)
    blocks, masks = gather_blocks(message)
    near = lax.ppermute(near, "gx", pairs(gx, 0))
    count = len(blocks)
    coefs, row = call(
        functools.partial(side_kernel, dims, rank_z), [((size, part), f32), ((8, lanes), f32)], [VM] * 3
    )(state, near, n)
    mixed_type, sums_type = ((size, width), f32), ((peers, lanes), f32)
    outs = [mixed_type, ((2 * nv, lanes), f32), sums_type]
    close = [blocks[i] for i in range(count - 1) if masks[i] in (0, 1)]
    others = [blocks[i] for i in range(count - 1) if masks[i] not in (0, 1)]
    (premixed,) = call(
        functools.partial(premix_kernel, dims, width, rank_x, len(close)), [mixed_type], [VM] * (len(close) + 1)
    )(message, *close)
    premixed, gap = call(
        functools.partial(second_premix_kernel, dims, width, rank_x, len(others)),
        [mixed_type, ((size, part), f32)],
        [VM] * (len(others) + 4),
    )(message, *others, premixed, coefs, u)
    mixing_args = (width, rank_x, masks)
    rest = (state, n, row, u)
    if basis_y.shape[0] * gy == basis_y.shape[1]:
        mixed, lack, sums = call(
            functools.partial(third_kernel, dims, rank_z, *mixing_args), outs, [VM] * (count + 6)
        )(*blocks, *rest, premixed, gap)
    else:
        mixed, lack = call(
            functools.partial(mix_kernel, dims, *mixing_args), outs[:2], [VM] * (count + 1)
        )(*blocks, premixed)
        mixed = mixed.reshape(rows_x, rows_y, width)
        core = lax.psum(jnp.einsum("xyk,yb->xbk", mixed, basis_y, precision=HIGH), "gy")
        mixed = jnp.einsum("xbk,yb->xyk", core, basis_y, precision=HIGH).reshape(size, width)
        (sums,) = call(functools.partial(settle_kernel, dims, rank_z), outs[2:], [VM] * 7)(mixed, lack, *rest, coefs)
    recon, state = call(functools.partial(decode_kernel, dims), [(block, f32)] * 2, [VM] * 5)(
        mixed, t, lack, near, state
    )
    if peers > 64:
        sums = lax.psum(sums[0], ("gx", "gy"))
    else:
        sums = jnp.sum(lax.all_to_all(sums, ("gx", "gy"), 0, 0, tiled=True), axis=0)
    residual = jnp.sqrt(sums[:nv] / (sums[nv : 2 * nv] + 1e-06))
    return (state.reshape(dims), recon.reshape(dims), residual)


def solution(mesh):
    return jax.shard_map(
        program,
        mesh=mesh,
        in_specs=(
            P(None, "gx", "gy", None),
            P(),
            P(),
            P(),
            P(),
            P("gx", None),
            P("gy", None),
            P(),
            P(),
        ),
        out_specs=(P(None, "gx", "gy", None), P(None, "gx", "gy", None), P()),
        check_vma=False,
    )
```

```python
import functools
import math

import jax
import jax.numpy as jnp
from jax import lax
from jax.experimental import pallas as pl
from jax.experimental.pallas import tpu as pltpu
from jax.sharding import PartitionSpec as P


HIGH = lax.Precision.HIGHEST
VM = pl.BlockSpec(memory_space=pltpu.VMEM)
SM = pl.BlockSpec(memory_space=pltpu.SMEM)


def call(kernel, outs, in_specs, scratch=(), vmem=12, out_specs=None):
    return pl.pallas_call(
        kernel,
        out_shape=[jax.ShapeDtypeStruct(s, d) for s, d in outs],
        in_specs=in_specs,
        out_specs=out_specs or [VM] * len(outs),
        scratch_shapes=list(scratch),
        compiler_params=pltpu.CompilerParams(vmem_limit_bytes=vmem << 20),
        cost_estimate=pl.CostEstimate(flops=10**7, bytes_accessed=10**6, transcendentals=0),
    )


def split(a):
    hi = a.astype(jnp.bfloat16)
    lo = (a - hi.astype(jnp.float32)).astype(jnp.bfloat16)
    return hi, lo


def mm(a, b, nt=False):
    dims = (((1,), (1 if nt else 0,)), ((), ()))
    return lax.dot_general(a, b, dims, preferred_element_type=jnp.float32)


def mm3(a, b, nt=False):
    return mm(a[0], b[0], nt) + mm(a[0], b[1], nt) + mm(a[1], b[0], nt)


def place(shape, dim):
    return lax.broadcasted_iota(jnp.int32, shape, dim)


def shifted(w, axis, before=0.0, after=0.0):
    size = w.shape[axis]
    pos = place(w.shape, axis)
    low = jnp.where(pos == 0, before, pltpu.roll(w, 1, axis))
    high = jnp.where(pos == size - 1, after, pltpu.roll(w, size - 1, axis))
    return low + high


def tiles_of(a):
    return a.reshape(a.size // (8 * a.shape[-1]), 8, a.shape[-1])


def reaction(ws, act, both, low):
    n = len(ws)
    cold = -math.log2(math.e) / (1.5 + jnp.tanh(ws[0]))
    rates = [tiles_of(jnp.exp2(act[v] * cold) * ws[v]) for v in range(n)]
    count, lanes = rates[0].shape[0], rates[0].shape[2]
    stacked = jnp.concatenate(
        [jnp.concatenate([rates[v][t] for v in range(n)], axis=0) for t in range(count)], axis=1
    )
    hi, lo = split(stacked)
    out = mm(both, jnp.concatenate([hi, lo], axis=0)) + mm(low, hi)
    return [
        jnp.stack([out[v * 8 : (v + 1) * 8, t * lanes : (t + 1) * lanes] for t in range(count)]).reshape(ws[v].shape)
        for v in range(n)
    ]


def stage(ref, nv, rows_x, rows_y, dif, act, mixers, emit, low_edge, high_edge, step=4):
    lanes = ref.shape[1]
    size = rows_x * rows_y

    def rows(v, x, n):
        return ref[pl.ds(v * size + x * rows_y, n * rows_y), :].reshape(n, rows_y, lanes)

    step = min(step, rows_x)
    for x in range(0, rows_x, step):
        ws = [rows(v, x, step) for v in range(nv)]
        made = reaction(ws, act, *mixers)
        for v in range(nv):
            w = ws[v]
            first = rows(v, x - 1, 1) if x > 0 else low_edge(v)[None]
            last = rows(v, x + step, 1) if x + step < rows_x else high_edge(v)[None]
            beside = jnp.concatenate([first, w[:-1]], 0) + jnp.concatenate([w[1:], last], 0)
            around = beside + shifted(w, 1) + shifted(w, 2)
            kept = (1.0 - 6.0 * dif[v]) * w
            emit(v, x, step, kept + (dif[v] * around + made[v]))


def odd(axis):
    return lax.axis_index(axis) % 2 == 1


def two(one, other, is_odd, at):
    a, b = one[at, :], other[at, :]
    return jnp.where(is_odd, a, b), jnp.where(is_odd, b, a)


def far_side():
    return odd("gx")


def pack_y_kernel(dims, f_ref, p1, p2):
    nv, rows_x, rows_y, _ = dims
    size = rows_x * rows_y
    for layer in range(2):
        for v in range(nv):
            low = f_ref[pl.ds(v * size + layer, rows_x, stride=rows_y), :]
            high = f_ref[pl.ds(v * size + rows_y - 1 - layer, rows_x, stride=rows_y), :]
            at = pl.ds((layer * nv + v) * rows_x, rows_x)
            p1[at, :] = jnp.where(odd("gy"), low, high)
            p2[at, :] = jnp.where(odd("gy"), high, low)


def pack_x_kernel(dims, f_ref, q1, q2):
    nv, rows_x, rows_y, _ = dims
    size = rows_x * rows_y
    for layer in range(2):
        for v in range(nv):
            low = f_ref[pl.ds(v * size + layer * rows_y, rows_y), :]
            high = f_ref[pl.ds(v * size + (rows_x - 1 - layer) * rows_y, rows_y), :]
            at = pl.ds((layer * nv + v) * rows_y, rows_y)
            q1[at, :] = jnp.where(odd("gx"), low, high)
            q2[at, :] = jnp.where(odd("gx"), high, low)


def first_kernel(dims, f_ref, x1, bz_ref, bv_ref, mix_ref, dif, pre, act, *outs):
    s_ref, k_ref, t_ref, u_ref, n_ref, both_ref, low_ref = outs
    nv, rows_x, rows_y, lanes = dims
    size = rows_x * rows_y
    spot = place((nv, nv), 1)
    scaled = mix_ref[...]
    for u in range(nv):
        scaled = jnp.where(spot == u, scaled * pre[u], scaled)
    wide = (nv * 8, nv)
    spread = (place(wide, 0) // 8 == place(wide, 1)).astype(jnp.float32)
    full = jnp.dot(spread, scaled, precision=HIGH, preferred_element_type=jnp.float32)
    full = lax.dot_general(
        full, spread, (((1,), (1,)), ((), ())), precision=HIGH, preferred_element_type=jnp.float32
    )
    hi, lo = split(jnp.where(place(full.shape, 0) % 8 == place(full.shape, 1) % 8, full, 0.0))
    both = jnp.concatenate([hi, hi], axis=1)
    both_ref[...], low_ref[...] = both, lo

    def emit(v, x, n, made):
        s_ref[pl.ds(v * size + x * rows_y, n * rows_y), :] = made.reshape(n * rows_y, lanes)

    def near(is_low):
        is_near = odd("gx") if is_low else jnp.logical_not(odd("gx"))
        return lambda v: jnp.where(is_near, x1[pl.ds(v * rows_y, rows_y), :], 0.0)

    stage(f_ref, nv, rows_x, rows_y, dif, act, (both, lo), emit, near(True), near(False))
    bz, bv = bz_ref[...], bv_ref[...]
    rank_z, rank_v = bz.shape[0], bv.shape[0]
    width, part = rank_z * rank_v, nv * rank_z
    pick_z = (place((rank_z, width), 1) % rank_z == place((rank_z, width), 0)).astype(jnp.float32)
    pick_v = (place((rank_v, width), 1) // rank_z == place((rank_v, width), 0)).astype(jnp.float32)
    first = (((0,), (0,)), ((), ()))
    wide_z = lax.dot_general(bz, pick_z, first, precision=HIGH, preferred_element_type=jnp.float32)
    wide_v = lax.dot_general(bv, pick_v, first, precision=HIGH, preferred_element_type=jnp.float32)
    for v in range(nv):
        product = wide_z * wide_v[v : v + 1, :]
        at = slice(v * lanes, (v + 1) * lanes)
        k_ref[0, at, :], k_ref[1, at, :] = split(product)
        t_ref[0, :, at], t_ref[1, :, at] = split(product.T)
    pick_u = (place((nv, part), 1) // rank_z == place((nv, part), 0)).astype(jnp.float32)
    tall = lax.dot_general(pick_v, bv, first, precision=HIGH, preferred_element_type=jnp.float32)
    tall = jnp.dot(tall, pick_u, precision=HIGH, preferred_element_type=jnp.float32)
    same = place((width, part), 0) % rank_z == place((width, part), 1) % rank_z
    u_ref[0], u_ref[1] = split(jnp.where(same, tall, 0.0))
    held = lanes // rank_z
    spread = (place((rank_z, lanes), 1) % rank_z == place((rank_z, lanes), 0)).astype(jnp.float32)
    wide_z = lax.dot_general(bz, spread, first, precision=HIGH, preferred_element_type=jnp.float32)
    group = place((lanes, lanes), 1) // rank_z
    for j in range(held):
        at = slice(j * lanes, (j + 1) * lanes)
        n_ref[0, at, :], n_ref[1, at, :] = split(jnp.where(group == j, wide_z, 0.0))


def second_kernel(
    dims, f_ref, s_ref, y1, y2, x1, x2, bx_ref, k_ref, both_ref, low_ref, dif, act,
    state_ref, m_ref, near_ref, sec, gy_ref, gx_ref,
):
    nv, rows_x, rows_y, lanes = dims
    size = rows_x * rows_y
    ix, iy = lax.axis_index("gx"), lax.axis_index("gy")
    has_x = (ix > 0, ix < lax.axis_size("gx") - 1)
    has_y = (iy > 0, iy < lax.axis_size("gy") - 1)
    mixers = (both_ref[...], low_ref[...])

    def y_ghost(layer, v):
        return jnp.stack(two(y1, y2, odd("gy"), pl.ds((layer * nv + v) * rows_x, rows_x)))

    def x_ghost(layer, v):
        return jnp.stack(two(x1, x2, odd("gx"), pl.ds((layer * nv + v) * rows_y, rows_y)))

    far = far_side()
    edges = (jnp.where(far, rows_x - 1, 0), jnp.where(far, 0, rows_x - 1))

    def keep(value, flags):
        inside = [jnp.where(flags[i], value[i], 0.0) for i in range(2)]
        return jnp.concatenate(inside, axis=0)

    ys = [y_ghost(0, v) for v in range(nv)]
    xs = [x_ghost(0, v) for v in range(nv)]
    made = reaction([jnp.concatenate([tiles_of(ys[v]), tiles_of(xs[v])], 0) for v in range(nv)], act, *mixers)
    for v in range(nv):
        g = ys[v]
        cut = g.size // (8 * lanes)
        low = f_ref[pl.ds(v * size, rows_x, stride=rows_y), :]
        high = f_ref[pl.ds(v * size + rows_y - 1, rows_x, stride=rows_y), :]
        lap = y_ghost(1, v) + jnp.stack([low, high]) - 6.0 * g
        lap = lap + shifted(g, 1) + shifted(g, 2)
        out = g + (dif[v] * lap + made[v][:cut].reshape(g.shape))
        gy_ref[pl.ds(v * 2 * rows_x, 2 * rows_x), :] = keep(out, has_y)
        sec[pl.ds(v * size, size), :] = s_ref[pl.ds(v * size, size), :]
        at = pl.ds(v * size, rows_x, stride=rows_y)
        sec[at, :] = sec[at, :] + dif[v] * g[0]
        at = pl.ds(v * size + rows_y - 1, rows_x, stride=rows_y)
        sec[at, :] = sec[at, :] + dif[v] * g[1]
        g = xs[v]
        low = f_ref[pl.ds(v * size, rows_y), :]
        high = f_ref[pl.ds(v * size + size - rows_y, rows_y), :]
        lap = x_ghost(1, v) + jnp.stack([low, high]) - 6.0 * g
        lap = lap + shifted(g, 1) + shifted(g, 2)
        out = g + (dif[v] * lap + made[v][cut:].reshape(g.shape))
        gx_ref[pl.ds(v * 2 * rows_y, 2 * rows_y), :] = keep(out, has_x)
        at = pl.ds(pl.multiple_of(v * size + edges[0] * rows_y, rows_y), rows_y)
        sec[at, :] = sec[at, :] + dif[v] * x2[pl.ds(v * rows_y, rows_y), :]

    def emit(v, x, n, made):
        at = pl.ds(v * size + x * rows_y, n * rows_y)
        state_ref[at, :] = 0.5 * (f_ref[at, :] + made.reshape(n * rows_y, lanes))

    stage(
        sec, nv, rows_x, rows_y, dif, act, mixers, emit,
        lambda v: gx_ref[pl.ds(v * 2 * rows_y, rows_y), :],
        lambda v: gx_ref[pl.ds((v * 2 + 1) * rows_y, rows_y), :],
    )
    total, his, los = 0.0, [], []
    spot = spots(dims, k_ref.shape[2], bx_ref.shape[1])[2]
    for v in range(nv):
        half = 0.5 * dif[v]
        at = pl.ds(v * size, rows_x, stride=rows_y)
        state_ref[at, :] = state_ref[at, :] + half * gy_ref[pl.ds(v * 2 * rows_x, rows_x), :]
        at = pl.ds(v * size + rows_y - 1, rows_x, stride=rows_y)
        state_ref[at, :] = state_ref[at, :] + half * gy_ref[pl.ds((v * 2 + 1) * rows_x, rows_x), :]
        rows = [state_ref[pl.ds(v * size, size), :]]
        for out, start, edge in ((m_ref, spot, edges[0]), (near_ref, 0, edges[1])):
            ends = [dif[v] * dif[v] * a for a in two(y1, y2, odd("gy"), pl.ds(v * rows_x + edge, 1))]
            for end in range(2):
                out[pl.ds(start + end * nv + v, 1), :] = ends[end]
            rows.append(ends_tile(*ends, rows_y))
        hi, lo = split(jnp.concatenate(rows, axis=0))
        his.append(hi)
        los.append(lo)
        if len(his) == 2 or v == nv - 1:
            at = pl.ds((v + 1 - len(his)) * lanes, len(his) * lanes)
            part = mm3((jnp.concatenate(his, 1), jnp.concatenate(los, 1)), (k_ref[0, at, :], k_ref[1, at, :]))
            total, his, los = total + part, [], []
    pack_message(dims, m_ref, total[:size], bx_ref[...], total[size:])


def ends_tile(first, last, rows):
    shape = (rows, first.shape[1])
    return jnp.where(place(shape, 0) == 0, first, jnp.where(place(shape, 0) == rows - 1, last, 0.0))


def spots(dims, width, rank_x):
    nv, rows_x, rows_y, lanes = dims
    size = rows_x * rows_y
    assert width % lanes * 2 == lanes and rank_x * 2 == lanes
    tail = width // lanes * size
    basis = tail + size // 2
    ends = basis + rows_x // 2
    made = ends + 2 * nv
    return tail, basis, ends, made, made + -(-(width // lanes * 4 + 2) // 8) * 8


def fold(a):
    half = a.shape[0] // 2
    return jnp.concatenate([a[:half], a[half:]], axis=1)


def unfold(a):
    half = a.shape[1] // 2
    return jnp.concatenate([a[:, :half], a[:, half:]], axis=0)


def pack_message(dims, m_ref, values, basis, ends):
    _, rows_x, rows_y, lanes = dims
    size, width = values.shape
    tail, base, _, made, _ = spots(dims, width, basis.shape[1])
    whole = width // lanes
    ends = [ends[row : row + 1] for row in (0, rows_y - 1, rows_y, 2 * rows_y - 1)]
    for i in range(whole):
        m_ref[pl.ds(i * size, size), :] = values[:, i * lanes : (i + 1) * lanes]
        for end in range(4):
            m_ref[pl.ds(made + 4 * i + end, 1), :] = ends[end][:, i * lanes : (i + 1) * lanes]
    m_ref[pl.ds(tail, size // 2), :] = fold(values[:, whole * lanes :])
    m_ref[pl.ds(base, rows_x // 2), :] = fold(basis)
    for end in range(0, 4, 2):
        rest = [ends[end][:, whole * lanes :], ends[end + 1][:, whole * lanes :]]
        m_ref[pl.ds(made + 4 * whole + end // 2, 1), :] = jnp.concatenate(rest, axis=1)


def unpack_message(dims, m_ref, width, rank_x):
    _, rows_x, rows_y, lanes = dims
    size = rows_x * rows_y
    tail, base, _, made, _ = spots(dims, width, rank_x)
    whole = width // lanes
    parts = [m_ref[pl.ds(i * size, size), :] for i in range(whole)]
    parts.append(unfold(m_ref[pl.ds(tail, size // 2), :]))
    basis = unfold(m_ref[pl.ds(base, rows_x // 2), :])
    half = lanes // 2
    ends = []
    for end in range(4):
        rest = m_ref[pl.ds(made + 4 * whole + end // 2, 1), :]
        rest = rest[:, end % 2 * half : (end % 2 + 1) * half]
        ends.append(jnp.concatenate([m_ref[pl.ds(made + 4 * i + end, 1), :] for i in range(whole)] + [rest], axis=1))
    tiles = ends_tile(*ends[:2], rows_y), ends_tile(*ends[2:], rows_y)
    return jnp.concatenate(parts, axis=1), basis, tiles


def from_far(me, masks, index, items):
    block = jnp.bitwise_xor(me, masks[index])
    far = jnp.where(block % 2 == 1, block + 1, block - 1)
    total = None
    mask = 3
    while mask < len(masks):
        other = masks.index(masks[index] ^ mask)
        item = jnp.where(far == jnp.bitwise_xor(block, mask), items[other], 0.0)
        total = item if total is None else total + item
        mask = 2 * mask + 1
    return total


def repeated(basis, rows_y):
    rows_x, rank_x = basis.shape
    return jnp.broadcast_to(basis[:, None, :], (rows_x, rows_y, rank_x)).reshape(rows_x * rows_y, rank_x)


def link_to(own, bases, rows_y):
    link = mm3(split(own), split(bases), True)
    return split(jnp.where(same_row(link, rows_y), link, 0.0))


def same_row(link, rows_y):
    return place(link.shape, 0) % rows_y == place(link.shape, 1) % rows_y


def mix_blocks(dims, width, rank_x, own_ref, refs):
    rows_y = dims[2]
    own = repeated(unpack_message(dims, own_ref, width, rank_x)[1], rows_y)
    parts = [unpack_message(dims, ref, width, rank_x) for ref in refs]
    values = jnp.concatenate([values for values, _, _ in parts], axis=0)
    bases = jnp.concatenate([repeated(basis, rows_y) for _, basis, _ in parts], axis=0)
    return mm3(link_to(own, bases, rows_y), split(values))


def premix_kernel(dims, width, rank_x, n, own_ref, *refs):
    refs[n][...] = mix_blocks(dims, width, rank_x, own_ref, refs[:n])


def second_premix_kernel(dims, width, rank_x, n, own_ref, *refs):
    d_ref, w_ref, u_ref, out_ref, gap_ref = refs[n:]
    mixed = d_ref[...] + mix_blocks(dims, width, rank_x, own_ref, refs[:n])
    out_ref[...] = mixed
    gap_ref[...] = w_ref[...] - mm3(split(mixed), (u_ref[0], u_ref[1]))


def last_values(dims, width, rank_x, masks, refs):
    _, rows_x, rows_y, _ = dims
    me = lax.axis_index("gx")
    parts = [unpack_message(dims, ref, width, rank_x) for ref in refs]
    values, bases = [parts[-1][0]], [repeated(parts[-1][1], rows_y)]
    for i, (_, basis, _) in enumerate(parts):
        last = jnp.bitwise_xor(me, masks[i]) % 2 == 1
        near = parts[masks.index(masks[i] ^ 1)][2][1]
        lacks = (from_far(me, masks, i, [ends[0] for _, _, ends in parts]), near)
        rows = (jnp.where(last, basis[rows_x - 1 :], basis[:1]), jnp.where(last, basis[:1], basis[rows_x - 1 :]))
        for lack, row in zip(lacks, rows):
            if lack is not None:
                values.append(lack)
                bases.append(jnp.broadcast_to(row, (rows_y, rank_x)))
    own = repeated(parts[0][1], rows_y)
    return split(jnp.concatenate(values, axis=0)), own, jnp.concatenate(bases, axis=0)


def squares(a):
    return jnp.sum((a * a).reshape(a.shape[0] // 8, 8, a.shape[1]), axis=0)


def zero_one(flags):
    return flags.astype(jnp.float32).astype(jnp.bfloat16)


def tally(outside, mass, lanes):
    hi, lo = split(jnp.concatenate(outside + mass, axis=0))
    ones = jnp.ones((8, lanes), jnp.bfloat16)
    hi, lo = split(mm(ones, hi, True) + mm(ones, lo, True))
    shape = (hi.shape[1], lanes)
    pick = zero_one(place(shape, 0) // 8 == place(shape, 1))
    return mm(hi, pick) + mm(lo, pick)


def outside_span(state, basis):
    coefs = mm3(split(state), basis)
    return coefs, state - mm3(split(coefs), basis, True)


def tile_of(ref, nv, v, rows_y):
    return ends_tile(ref[pl.ds(v, 1), :], ref[pl.ds(nv + v, 1), :], rows_y)


def side_kernel(dims, rank_z, state_ref, near_ref, n_ref, w_ref, row_ref):
    nv, rows_x, rows_y, lanes = dims
    size = rows_x * rows_y
    held = lanes // rank_z
    last = far_side()
    outside, mass = [], []
    for v in range(0, nv, held):
        state = jnp.concatenate([state_ref[pl.ds((v + j) * size, size), :] for j in range(held)], axis=1)
        near = jnp.concatenate([tile_of(near_ref, nv, v + j, rows_y) for j in range(held)], axis=1)
        top = jnp.where(last, state[:rows_y] + near, 0.0)
        bottom = jnp.where(last, 0.0, state[size - rows_y :] + near)
        state = jnp.concatenate([top, state[rows_y : size - rows_y], bottom], axis=0)
        coefs, rest = outside_span(state, (n_ref[0], n_ref[1]))
        w_ref[:, (v // held) * lanes : (v // held + 1) * lanes] = coefs
        for j in range(held):
            outside.append(squares(rest[:, j * lanes : (j + 1) * lanes]))
            mass.append(squares(state[:, j * lanes : (j + 1) * lanes]))
    row_ref[...] = tally(outside, mass, lanes)


def edge_state(dims, rank_z, state_ref, lack):
    nv, rows_x, rows_y, lanes = dims
    start = jnp.where(far_side(), (rows_x - 1) * rows_y, 0)
    held = lanes // rank_z
    whole = []
    for v in range(nv):
        at = pl.ds(pl.multiple_of(v * rows_x * rows_y + start, rows_y), rows_y)
        ends = [lack[end * nv + v : end * nv + v + 1] for end in range(2)]
        whole.append(state_ref[at, :] + ends_tile(*ends, rows_y))
    packed = [jnp.concatenate(whole[v : v + held], axis=1) for v in range(0, nv, held)]
    return whole, jnp.concatenate(packed, axis=0)


def edge_sums(dims, rank_z, whole, rest):
    nv, _, rows_y, lanes = dims
    held = lanes // rank_z
    outside = []
    for v in range(nv):
        i, j = divmod(v, held)
        outside.append(squares(rest[i * rows_y : (i + 1) * rows_y, j * lanes : (j + 1) * lanes]))
    return tally(outside, [squares(a) for a in whole], lanes)[0:1, :]


def edge_coefs(rows_y, coefs):
    count = coefs.shape[0] // rows_y
    return jnp.concatenate([coefs[i * rows_y : (i + 1) * rows_y] for i in range(count)], axis=1)


def put_edge(w, coefs):
    rows_y, last = coefs.shape[0], far_side()
    size = w.shape[0]
    top = w[:rows_y] + jnp.where(last, 0.0, coefs)
    bottom = w[size - rows_y :] + jnp.where(last, coefs, 0.0)
    return jnp.concatenate([top, w[rows_y : size - rows_y], bottom], axis=0)


def total_sums(gap, rows, sums_ref, rank_z):
    hi, lo = split(squares(gap))
    shape = (gap.shape[1], sums_ref.shape[1])
    pick = zero_one(place(shape, 0) // rank_z == place(shape, 1))
    row = jnp.sum(mm(hi, pick) + mm(lo, pick), axis=0, keepdims=True) + rows[0] + rows[1]
    sums_ref[...] = jnp.broadcast_to(row, sums_ref.shape)


def find_lack(dims, width, rank_x, masks, refs):
    spot = spots(dims, width, rank_x)[2]
    rows = [ref[pl.ds(spot, 2 * dims[0]), :] for ref in refs]
    lack = from_far(lax.axis_index("gx"), masks, 0, rows)
    return jnp.zeros_like(rows[0]) if lack is None else lack


def third_kernel(dims, rank_z, width, rank_x, masks, *refs):
    n = len(masks)
    state_ref, n_ref, row_ref, u_ref, gap_ref, lack_ref, sums_ref = refs[n:]
    rows_y = dims[2]
    values, own, bases = last_values(dims, width, rank_x, masks, refs[:n])
    lack = find_lack(dims, width, rank_x, masks, refs[:n])
    whole, edge = edge_state(dims, rank_z, state_ref, lack)
    basis = (n_ref[0], n_ref[1])
    link = mm3(split(own), split(bases), True)
    coefs = mm3(split(edge), basis)
    spread = mm3(values, (u_ref[0], u_ref[1]))
    link = split(jnp.where(same_row(link, rows_y), link, 0.0))
    rest = edge - mm3(split(coefs), basis, True)
    gap = mm3(link, split(spread))
    row = edge_sums(dims, rank_z, whole, rest)
    gap = put_edge(gap_ref[...], edge_coefs(rows_y, coefs)) - gap
    total_sums(gap, (row_ref[0:1, :], row), sums_ref, rank_z)
    lack_ref[...] = lack


def mix_kernel(dims, width, rank_x, masks, *refs):
    n = len(masks)
    part_ref, d_ref, lack_ref = refs[n:]
    lack_ref[...] = find_lack(dims, width, rank_x, masks, refs[:n])
    values, own, bases = last_values(dims, width, rank_x, masks, refs[:n])
    d_ref[...] = part_ref[...] + mm3(link_to(own, bases, dims[2]), values)


def settle_kernel(dims, rank_z, d_ref, lack_ref, state_ref, n_ref, row_ref, u_ref, w_ref, sums_ref):
    whole, edge = edge_state(dims, rank_z, state_ref, lack_ref[...])
    coefs, rest = outside_span(edge, (n_ref[0], n_ref[1]))
    row = edge_sums(dims, rank_z, whole, rest)
    gap = put_edge(w_ref[...], edge_coefs(dims[2], coefs)) - mm3(split(d_ref[...]), (u_ref[0], u_ref[1]))
    total_sums(gap, (row_ref[0:1, :], row), sums_ref, rank_z)


def decode_into(dims, mixed, t_ref, lack_ref, near_ref, state_ref, recon_ref, out_ref):
    nv, rows_x, rows_y, lanes = dims
    size = rows_x * rows_y
    halves = split(mixed)
    far = far_side()
    starts = (jnp.where(far, size - rows_y, 0), jnp.where(far, 0, size - rows_y))
    for v in range(nv):
        whole = pl.ds(v * size, size)
        out_ref[whole, :] = state_ref[whole, :]
        for start, ref in zip(starts, (lack_ref, near_ref)):
            at = pl.ds(pl.multiple_of(v * size + start, rows_y), rows_y)
            out_ref[at, :] = state_ref[at, :] + tile_of(ref, nv, v, rows_y)
        cols = slice(v * lanes, (v + 1) * lanes)
        recon_ref[whole, :] = mm3(halves, (t_ref[0, :, cols], t_ref[1, :, cols]))


def decode_kernel(dims, d_ref, *refs):
    decode_into(dims, d_ref[...], *refs)


def finish_kernel(dims, width, rank_x, masks, *refs):
    n = len(masks)
    values, own, bases = last_values(dims, width, rank_x, masks, refs[:n])
    decode_into(dims, refs[n][...] + mm3(link_to(own, bases, dims[2]), values), *refs[n + 1 :])


def pairs(n, first):
    swaps = [(i, i + 1) for i in range(first, n - 1, 2)]
    return swaps + [(j, i) for i, j in swaps]


def gather_blocks(block):
    n = lax.axis_size("gx")
    assert n & (n - 1) == 0
    blocks, masks = [block], [0]
    bit = n // 2
    while bit:
        swaps = [(i, i ^ bit) for i in range(n)]
        blocks = blocks + [lax.ppermute(b, "gx", swaps) for b in blocks]
        masks = masks + [mask ^ bit for mask in masks]
        bit //= 2
    return blocks, tuple(masks)


def program(field, diffusion, prefactor, activation, mixing, basis_x, basis_y, basis_z, basis_v):
    f32, bf16 = jnp.float32, jnp.bfloat16
    dims = field.shape
    nv, rows_x, rows_y, lanes = dims
    size = rows_x * rows_y
    rank_x, rank_z, rank_v = basis_x.shape[1], basis_z.shape[1], basis_v.shape[1]
    width, part = rank_z * rank_v, nv * rank_z
    gx, gy = lax.axis_size("gx"), lax.axis_size("gy")
    peers = gx * gy
    flat = field.reshape(nv * size, lanes)
    block = (nv * size, lanes)

    y_msg, x_msg = (2 * nv * rows_x, lanes), (2 * nv * rows_y, lanes)
    p1, p2 = call(functools.partial(pack_y_kernel, dims), [(y_msg, f32)] * 2, [VM])(flat)
    y1 = lax.ppermute(p1, "gy", pairs(gy, 0))
    y2 = lax.ppermute(p2, "gy", pairs(gy, 1))
    q1, q2 = call(functools.partial(pack_x_kernel, dims), [(x_msg, f32)] * 2, [VM])(flat)
    x2 = lax.ppermute(q2, "gx", pairs(gx, 1))
    x1 = lax.ppermute(q1, "gx", pairs(gx, 0))

    section, k, t, u, n, both, low = call(
        functools.partial(first_kernel, dims),
        [
            (block, f32),
            ((2, nv * lanes, width), bf16),
            ((2, width, nv * lanes), bf16),
            ((2, width, part), bf16),
            ((2, lanes // rank_z * lanes, lanes), bf16),
            ((nv * 8, nv * 16), bf16),
            ((nv * 8, nv * 8), bf16),
        ],
        [VM] * 5 + [SM] * 3,
    )(flat, x1, basis_z.T, basis_v.T, mixing, diffusion, prefactor, activation)
    state, message, near = call(
        functools.partial(second_kernel, dims),
        [(block, f32), ((spots(dims, width, rank_x)[4], lanes), f32), ((2 * nv, lanes), f32)],
        [VM] * 10 + [SM] * 2,
        [
            pltpu.VMEM(block, f32),
            pltpu.VMEM((nv * 2 * rows_x, lanes), f32),
            pltpu.VMEM((nv * 2 * rows_y, lanes), f32),
        ],
    )(flat, section, y1, y2, x1, x2, basis_x, k, both, low, diffusion, activation)
    blocks, masks = gather_blocks(message)
    near = lax.ppermute(near, "gx", pairs(gx, 0))
    count = len(blocks)
    coefs, row = call(
        functools.partial(side_kernel, dims, rank_z), [((size, part), f32), ((8, lanes), f32)], [VM] * 3
    )(state, near, n)
    mixed_type, sums_type = ((size, width), f32), ((peers, lanes), f32)
    outs = [mixed_type, ((2 * nv, lanes), f32), sums_type]
    close = [blocks[i] for i in range(count - 1) if masks[i] in (0, 1)]
    others = [blocks[i] for i in range(count - 1) if masks[i] not in (0, 1)]
    (premixed,) = call(
        functools.partial(premix_kernel, dims, width, rank_x, len(close)), [mixed_type], [VM] * (len(close) + 1)
    )(message, *close)
    premixed, gap = call(
        functools.partial(second_premix_kernel, dims, width, rank_x, len(others)),
        [mixed_type, ((size, part), f32)],
        [VM] * (len(others) + 4),
    )(message, *others, premixed, coefs, u)
    mixing_args = (width, rank_x, masks)
    rest = (state, n, row, u)
    if basis_y.shape[0] * gy == basis_y.shape[1]:
        lack, sums = call(
            functools.partial(third_kernel, dims, rank_z, *mixing_args), outs[1:], [VM] * (count + 5)
        )(*blocks, *rest, gap)
        decode, given = functools.partial(finish_kernel, dims, *mixing_args), (*blocks, premixed)
    else:
        mixed, lack = call(
            functools.partial(mix_kernel, dims, *mixing_args), outs[:2], [VM] * (count + 1)
        )(*blocks, premixed)
        mixed = mixed.reshape(rows_x, rows_y, width)
        core = lax.psum(jnp.einsum("xyk,yb->xbk", mixed, basis_y, precision=HIGH), "gy")
        mixed = jnp.einsum("xbk,yb->xyk", core, basis_y, precision=HIGH).reshape(size, width)
        (sums,) = call(functools.partial(settle_kernel, dims, rank_z), outs[2:], [VM] * 7)(mixed, lack, *rest, coefs)
        decode, given = functools.partial(decode_kernel, dims), (mixed,)
    recon, state = call(decode, [(block, f32)] * 2, [VM] * (len(given) + 4))(
        *given, t, lack, near, state
    )
    if peers > 64:
        sums = lax.psum(sums[0], ("gx", "gy"))
    else:
        sums = jnp.sum(lax.all_to_all(sums, ("gx", "gy"), 0, 0, tiled=True), axis=0)
    residual = jnp.sqrt(sums[:nv] / (sums[nv : 2 * nv] + 1e-06))
    return (state.reshape(dims), recon.reshape(dims), residual)


def solution(mesh):
    return jax.shard_map(
        program,
        mesh=mesh,
        in_specs=(
            P(None, "gx", "gy", None),
            P(),
            P(),
            P(),
            P(),
            P("gx", None),
            P("gy", None),
            P(),
            P(),
        ),
        out_specs=(P(None, "gx", "gy", None), P(None, "gx", "gy", None), P()),
        check_vma=False,
    )
```
